128 devices in a mesh: lang: 8 (over z, y_lo), fsdp: 16 (over y_hi, x, core).
Axes of the slice: x: 4, y: 4 (y_hi: 2, y_lo: 2; y = y_hi * 2 + y_lo), z: 4, core: 2. Of those that a mesh axis runs over, the one named last changes fastest.
Arguments:
- tokens: bfloat16 [8, 768, 8192], P('lang', 'fsdp'), may hold values from -6 to 6
- grad_out: bfloat16 [8, 768, 8192], P('lang', 'fsdp'), may hold values from -24 to 24
- doc_ids: int32 [8, 768], P('lang'), may hold values from 0 to 95, never falling along the last dimension, each value on 1 to 64 neighbouring positions
- w_gate: bfloat16 [8192, 4096], P(None, 'fsdp'), may hold values from -0.0625 to 0.0625
- w_up: bfloat16 [8192, 4096], P(None, 'fsdp'), may hold values from -0.0625 to 0.0625
- w_down: bfloat16 [4096, 8192], P('fsdp'), may hold values from -0.09375 to 0.09375
Outputs:
- grad_tokens: bfloat16 [8, 768, 8192], P('lang', 'fsdp')
- grad_gate: bfloat16 [8192, 4096], P('lang', 'fsdp')
- grad_up: bfloat16 [8192, 4096], P('lang', 'fsdp')
- grad_down: bfloat16 [4096, 8192], P('fsdp', 'lang')
The draws below stay inside these ranges and needn't reach their ends.
Inputs may be any that keep to these rules, and one draw needn't show every extreme that they name: `doc_ids`: document numbers never fall along a group's pack.
All inputs are finite; a program needn't handle non-finite values.
Results may differ from the reference program's by a relative error of at most 0.015.
Values may be sent and summed in bfloat16 or wider, within the bound.
No kernel may reach another device: no remote copies, remote signals or barrier semaphores. Data moves between devices by JAX's collectives and lax.ppermute only.
A program may use at most 192 MiB of HBM per device.

```python
import math
import jax
import jax.numpy as jnp
import numpy as np
from jax import lax

D = 8192
HID_DEV = 256
LANGS = 8
HS = 4096
TL = 768
DOCS = 96
DOC_MOST = 64
N_FSDP = 16


def draw_grad_out(key, part):
    ladder = jnp.arange(LANGS, dtype=jnp.float32) / max(LANGS - 1, 1)
    scales = jnp.exp(ladder * jnp.log(3.0))
    values = jax.random.normal(key, (LANGS, TL, D), jnp.float32)
    values = jnp.clip(values * scales[:, None, None], -24.0, 24.0)
    return values.astype(jnp.bfloat16)


def block_scale(own_key, extent, pieces, low, largest):
    loudness = 1.0
    for position, shards_of in pieces:
        draws = jax.random.uniform(jax.random.fold_in(jax.random.fold_in(own_key, 6), position), (shards_of,), jnp.float32, low / len(pieces), largest / len(pieces))
        loudness = loudness * jnp.repeat(jnp.exp(draws), extent[position] // shards_of).reshape((-1,) + (1,) * (len(extent) - 1 - position))
    return loudness


def profile(count, total, reach, lean):
    portions = [(1 << 20) // math.isqrt(rank ** lean) + 1 for rank in range(2, count + 1)]
    rest, given = total - reach - (count - 1), [1] * (count - 1)
    while rest > 0:
        movable = [i for i in range(count - 1) if given[i] < reach]
        mass, left = sum([portions[i] for i in movable]), rest
        for i in movable:
            addition = min(reach - given[i], max(1, left * portions[i] // mass), rest)
            given[i] = given[i] + addition
            rest = rest - addition
    return np.array([reach] + given)


def ragged(stream_key, number_of, total, limit, skew):
    if number_of == 2:
        one = jax.random.randint(stream_key, (), max(1, total - limit), min(limit, total - 1) + 1)
        return jnp.stack([one, total - one])
    sizes = jnp.asarray(profile(number_of, total, limit, skew), jnp.int32)
    twos = (number_of - 1) // 2
    source_of, sink = sizes[1:1 + 2 * twos:2], sizes[2:2 + 2 * twos:2]
    slack = jnp.minimum(source_of - 1, limit - sink)
    shifted = jax.random.randint(jax.random.fold_in(stream_key, 1), (twos,), 0, 1 << 20) % (slack + 1)
    sizes = sizes.at[1:1 + 2 * twos:2].set(source_of - shifted).at[2:2 + 2 * twos:2].set(sink + shifted)
    return sizes[jax.random.permutation(jax.random.fold_in(stream_key, 2), number_of)]


def noise(key, dims, scale, limit, shards=(), kind=jnp.bfloat16):
    result = jax.random.normal(key, dims, jnp.float32) * scale
    if len(shards) > 0:
        result = block_scale(key, dims, shards, -0.22, 0.18) * result
    return jnp.clip(result, min=-limit, max=limit).astype(kind)


def setup_inputs(seed: int = 0) -> dict:
    seeds = jax.random.split(jax.random.key(seed), 7)
    tokens = noise(seeds[0], (LANGS, TL, D), 1.0, 6.0, ((0, 8), (1, 16)))
    grad_out = draw_grad_out(jax.random.fold_in(seeds[6], 71), 0)
    doc_ids = jax.vmap(lambda own: jnp.searchsorted(jnp.cumsum(ragged(own, DOCS, TL, DOC_MOST, 2)), jnp.arange(TL), side="right"))(jax.random.split(seeds[2], LANGS)).reshape((LANGS, TL)).astype(jnp.int32)
    w_gate = noise(seeds[3], (D, HS), D ** -0.5, 0.0625, ((1, 16),))
    w_up = noise(seeds[4], (D, HS), D ** -0.5, 0.0625, ((1, 16),))
    w_down = noise(seeds[5], (HS, D), HS ** -0.5, 0.09375, ((0, 16),))
    return {"tokens": tokens, "grad_out": grad_out, "doc_ids": doc_ids, "w_gate": w_gate, "w_up": w_up, "w_down": w_down}


epsilon = 1e-6


def contract_rows(left, right):
    return lax.dot_general(left, right, (((0,), (0,)), ((), ())), preferred_element_type=jnp.float32)


def contract_cols(left, right):
    return lax.dot_general(left, right, (((1,), (1,)), ((), ())), preferred_element_type=jnp.float32)


def forward_parts(features, upstream, segment, w_gate, w_up, w_down):
    counts = jnp.sum((segment[:, None] == segment[None, :]).astype(jnp.float32), axis=1)
    inverse = 1.0 / counts
    gate_pre = jnp.dot(features, w_gate, preferred_element_type=jnp.float32)
    up_pre = jnp.dot(features, w_up, preferred_element_type=jnp.float32)
    gate_sig = jax.nn.sigmoid(gate_pre)
    activated = gate_pre * gate_sig
    hidden = (activated * up_pre * inverse[:, None]).astype(jnp.bfloat16)
    hid_grad = contract_cols(upstream, w_down) * inverse[:, None]
    gate_grad = (hid_grad * up_pre * gate_sig * (1.0 + gate_pre * (1.0 - gate_sig))).astype(jnp.bfloat16)
    up_grad = (hid_grad * activated).astype(jnp.bfloat16)
    return hidden, gate_grad, up_grad


def reference(tokens, grad_out, doc_ids, w_gate, w_up, w_down):
    input_grads = []
    saved = []
    ratio_list = []
    for language in range(LANGS):
        features = tokens[language]
        upstream = grad_out[language]
        hidden, gate_grad, up_grad = forward_parts(features, upstream, doc_ids[language], w_gate, w_up, w_down)
        summed = jnp.zeros((TL, D), jnp.float32)
        for column_block in range(N_FSDP):
            lower = column_block * HID_DEV
            upper = lower + HID_DEV
            partial_sum = contract_cols(gate_grad[:, lower:upper], w_gate[:, lower:upper])
            partial_sum = partial_sum + contract_cols(up_grad[:, lower:upper], w_up[:, lower:upper])
            rounded = lax.optimization_barrier(partial_sum.astype(jnp.bfloat16))
            summed = summed + rounded.astype(jnp.float32)
        input_grads.append(summed.astype(jnp.bfloat16))
        g_gate = contract_rows(features, gate_grad)
        g_up = contract_rows(features, up_grad)
        g_down = contract_rows(upstream, hidden)
        moment = (jnp.sum(g_gate * g_gate, axis=0) + jnp.sum(g_up * g_up, axis=0) + jnp.sum(g_down * g_down, axis=0)) / (3.0 * D) + epsilon
        ratio_list.append(1.0 / moment)
        saved.append((hidden, gate_grad, up_grad))
    ratios = jnp.stack(ratio_list)
    summed_ratio = jnp.sum(ratios, axis=0)
    acc_gate = jnp.zeros((D, HS), jnp.float32)
    acc_up = jnp.zeros((D, HS), jnp.float32)
    acc_down = jnp.zeros((D, HS), jnp.float32)
    for language in range(LANGS):
        hidden, gate_grad, up_grad = saved[language]
        weight_row = (ratios[language] / summed_ratio)[None, :]
        term_gate = lax.optimization_barrier((contract_rows(tokens[language], gate_grad) * weight_row).astype(jnp.bfloat16))
        term_up = lax.optimization_barrier((contract_rows(tokens[language], up_grad) * weight_row).astype(jnp.bfloat16))
        term_down = lax.optimization_barrier((contract_rows(grad_out[language], hidden) * weight_row).astype(jnp.bfloat16))
        acc_gate = acc_gate + term_gate.astype(jnp.float32)
        acc_up = acc_up + term_up.astype(jnp.float32)
        acc_down = acc_down + term_down.astype(jnp.float32)
    grad_tokens = jnp.stack(input_grads)
    return grad_tokens, acc_gate.astype(jnp.bfloat16), acc_up.astype(jnp.bfloat16), acc_down.T.astype(jnp.bfloat16)
```

```python
import functools

import jax
import jax.numpy as jnp
from jax import lax
from jax.experimental import pallas as pl
from jax.experimental.pallas import tpu as pltpu
from jax.sharding import PartitionSpec as P

epsilon = 1e-06
INTERPRET = False

PLACES = ((0, 0), (-1, 0), (1, 0), (0, 1), (-1, 1), (1, 1), (2, 0), (2, 1))
BATCHES = ((0, 1, 2, 3), (4, 5, 6), (7,))
PIECES = (
    (2, 1, 0), (2, 1, 1), (1, 1, 1), (-1, 1, 0), (1, 1, 0), (-1, 1, 1), (2, 0, 0), (2, 0, 1),
    (1, 0, 0), (1, 0, 1), (-1, 0, 0), (-1, 0, 1), (0, 1, 0), (0, 1, 1), (0, 0, 0), (0, 0, 1),
)


def fsdp_pairs(dx, dy, dc):
    return [
        (y * 8 + x * 2 + c, (y ^ dy) * 8 + (x + dx) % 4 * 2 + (c ^ dc))
        for y in range(2)
        for x in range(4)
        for c in range(2)
    ]


def lang_pairs(dz, dy):
    return [(z * 2 + y, (z + dz) % 4 * 2 + (y ^ dy)) for z in range(4) for y in range(2)]


def to_x(value, step):
    return lax.ppermute(value, "fsdp", fsdp_pairs(step, 0, 0))


def to_y_half(value):
    return lax.ppermute(value, "fsdp", fsdp_pairs(0, 1, 0))


def to_core(value):
    return lax.ppermute(value, "fsdp", fsdp_pairs(0, 0, 1))


def to_z(value, step):
    return lax.ppermute(value, "lang", lang_pairs(step, 0))


def to_y_next(value):
    return lax.ppermute(value, "lang", lang_pairs(0, 1))


def forward_kernel(tok, tok_p, out, out_p, wg, wu, wd, inv, ggu_ref, hid_ref, gate, up, back):
    step = pl.program_id(0)
    features = jnp.concatenate([tok[...], tok_p[...]], axis=0)
    upstream = jnp.concatenate([out[...], out_p[...]], axis=0)

    @pl.when(step == 0)
    def _():
        gate[...] = jnp.zeros_like(gate)
        up[...] = jnp.zeros_like(up)
        back[...] = jnp.zeros_like(back)

    gate[...] += jnp.dot(features, wg[...], preferred_element_type=jnp.float32)
    up[...] += jnp.dot(features, wu[...], preferred_element_type=jnp.float32)
    back[...] += lax.dot_general(
        upstream, wd[...], (((1,), (1,)), ((), ())), preferred_element_type=jnp.float32
    )

    @pl.when(step == pl.num_programs(0) - 1)
    def _():
        width = gate.shape[1]
        inverse = inv[...]
        gate_pre = gate[...]
        up_pre = up[...]
        sig = 1.0 / (1.0 + jnp.exp(-gate_pre))
        act = gate_pre * sig
        hid_ref[...] = (act * up_pre * inverse).astype(hid_ref.dtype)
        hid_grad = back[...] * inverse
        gate_grad = hid_grad * up_pre * sig * (1.0 + gate_pre * (1.0 - sig))
        ggu_ref[:, :width] = gate_grad.astype(ggu_ref.dtype)
        ggu_ref[:, width:] = (hid_grad * act).astype(ggu_ref.dtype)


def forward(tok, tok_p, out, out_p, w_gate, w_up, w_down, inverse):
    rows, depth = tok.shape
    hid = w_gate.shape[1]
    block = min(1024, depth)
    act = pl.BlockSpec((rows, block), lambda k: (0, k))
    wide = pl.BlockSpec((block, hid), lambda k: (k, 0))
    return pl.pallas_call(
        forward_kernel,
        name="forward",
        grid=(depth // block,),
        in_specs=[act, act, act, act, wide, wide,
                  pl.BlockSpec((hid, block), lambda k: (0, k)),
                  pl.BlockSpec((2 * rows, 1), lambda k: (0, 0))],
        out_specs=[pl.BlockSpec((2 * rows, 2 * hid), lambda k: (0, 0)),
                   pl.BlockSpec((2 * rows, hid), lambda k: (0, 0))],
        out_shape=[jax.ShapeDtypeStruct((2 * rows, 2 * hid), jnp.bfloat16),
                   jax.ShapeDtypeStruct((2 * rows, hid), jnp.bfloat16)],
        scratch_shapes=[pltpu.VMEM((2 * rows, hid), jnp.float32)] * 3,
        compiler_params=pltpu.CompilerParams(
            dimension_semantics=("arbitrary",), vmem_limit_bytes=24 << 20),
        interpret=INTERPRET,
    )(tok, tok_p, out, out_p, w_gate, w_up, w_down, inverse)


def gradient_kernel(n, depth, place, *refs):
    toks, outs = refs[: 2 * n], refs[2 * n : 4 * n]
    ggus, hids = refs[4 * n : 5 * n], refs[5 * n : 6 * n]
    pieces, ratio, ggu_t, hid_t, moment = refs[6 * n :]
    step = pl.program_id(0)
    hid = hid_t.shape[0]

    @pl.when(step == 0)
    def _():
        ggu = jnp.concatenate([r[...] for r in ggus], axis=0).astype(jnp.float32)
        ggu_t[...] = ggu.T.astype(ggu_t.dtype)
        hidden = jnp.concatenate([r[...] for r in hids], axis=0).astype(jnp.float32)
        hid_t[...] = hidden.T.astype(hid_t.dtype)
        moment[...] = jnp.zeros_like(moment)

    features = jnp.concatenate([r[...] for r in toks], axis=0)
    upstream = jnp.concatenate([r[...] for r in outs], axis=0)
    first = jnp.dot(ggu_t[...], features, preferred_element_type=jnp.float32)
    pieces[0, : 2 * hid] = first.astype(pieces.dtype)
    second = jnp.dot(hid_t[...], upstream, preferred_element_type=jnp.float32)
    pieces[0, 2 * hid :] = second.astype(pieces.dtype)
    lanes = moment.shape[1]
    total = jnp.zeros(moment.shape, jnp.float32)
    for i in range(0, first.shape[1], lanes):
        a = first[:hid, i : i + lanes]
        b = first[hid:, i : i + lanes]
        c = second[:, i : i + lanes]
        total += a * a + b * b + c * c
    moment[...] += total

    @pl.when(step == pl.num_programs(0) - 1)
    def _():
        summed = jnp.sum(moment[...], axis=1, keepdims=True) / (3.0 * depth) + epsilon
        ratio[...] = jnp.broadcast_to(1.0 / summed, ratio.shape)


def gradients(place, toks, outs, ggus, hids):
    n = len(ggus)
    depth = toks[0].shape[1]
    hid = hids[0].shape[1]
    tokens = sum(t.shape[0] for t in toks)
    block = depth // len(PIECES)
    lanes = min(128, block)
    acts = [pl.BlockSpec((a.shape[0], block), lambda k, p: (0, p[k])) for a in (*toks, *outs)]
    whole = [pl.BlockSpec(a.shape, lambda k, p: (0, 0)) for a in (*ggus, *hids)]
    return pl.pallas_call(
        functools.partial(gradient_kernel, n, depth),
        name="gradients",
        grid_spec=pltpu.PrefetchScalarGridSpec(
            num_scalar_prefetch=1,
            grid=(len(PIECES),),
            in_specs=acts + whole,
            out_specs=[pl.BlockSpec((1, 3 * hid, block), lambda k, p: (k, 0, 0)),
                       pl.BlockSpec((hid, 128), lambda k, p: (0, 0))],
            scratch_shapes=[pltpu.VMEM((2 * hid, tokens), jnp.bfloat16),
                            pltpu.VMEM((hid, tokens), jnp.bfloat16),
                            pltpu.VMEM((hid, lanes), jnp.float32)],
        ),
        out_shape=[jax.ShapeDtypeStruct((len(PIECES), 3 * hid, block), jnp.bfloat16),
                   jax.ShapeDtypeStruct((hid, 128), jnp.float32)],
        compiler_params=pltpu.CompilerParams(
            dimension_semantics=("arbitrary",), vmem_limit_bytes=24 << 20),
        interpret=INTERPRET,
    )(place, *toks, *outs, *ggus, *hids)


def contract_cols(left, right):
    return lax.dot_general(
        left, right, (((1,), (1,)), ((), ())), preferred_element_type=jnp.float32
    )


def bf(value):
    return value.astype(jnp.bfloat16)


def f32(value):
    return value.astype(jnp.float32)


def body(tokens, grad_out, doc_ids, w_gate, w_up, w_down):
    rows = tokens.shape[1]
    hid = w_gate.shape[1]
    lang, fsdp = lax.axis_index("lang"), lax.axis_index("fsdp")
    z, y_lo = lang // 2, lang % 2
    y_hi, x, core = fsdp // 8, fsdp // 2 % 4, fsdp % 2

    t, o = {}, {}
    t[0], o[0] = tokens[0], grad_out[0]
    t[1], o[1] = to_x(t[0], 1), to_x(o[0], 1)
    t[2], o[2] = to_x(t[0], -1), to_x(o[0], -1)
    t[3], o[3] = to_y_half(t[0]), to_y_half(o[0])
    t[4], o[5] = to_y_half(t[1]), to_y_half(o[2])
    t[6], o[6] = to_x(t[1], 1), to_x(o[2], -1)
    o[4], t[5] = to_x(o[3], 1), to_x(t[3], -1)
    t[7], o[7] = to_x(t[4], 1), to_x(o[5], -1)

    segment = doc_ids[0]
    counts = jnp.sum((segment[:, None] == segment[None, :]).astype(jnp.float32), axis=1)
    inverse = (1.0 / counts).reshape(16, rows)
    order = [(k, dc) for batch in BATCHES for dc in (0, 1) for k in batch]
    source = jnp.stack(
        [(y_hi ^ PLACES[k][1]) * 8 + (x + PLACES[k][0]) % 4 * 2 + (core ^ dc) for k, dc in order]
    )
    chosen = source[:, None] == jnp.arange(16)[None, :]
    inverse = jnp.sum(jnp.where(chosen[:, :, None], inverse[None], 0.0), axis=1)
    inverse = inverse.reshape(16 * rows, 1)
    both = jnp.concatenate([w_gate, w_up], axis=1)

    toks, outs, ggus, hids, part = [], [], [], [], {}
    at = 0
    for batch in BATCHES:
        size = rows * len(batch)
        tok = jnp.concatenate([t[k] for k in batch], axis=0)
        out = jnp.concatenate([o[k] for k in batch], axis=0)
        tok_p, out_p = to_core(tok), to_core(out)
        ggu, hidden = forward(
            tok, tok_p, out, out_p, w_gate, w_up, w_down, inverse[at : at + 2 * size]
        )
        at += 2 * size
        toks += [tok, tok_p]
        outs += [out, out_p]
        ggus.append(ggu)
        hids.append(hidden)

    target = jnp.stack([((z + dz) % 4 * 2 + (y_lo ^ dy)) * 2 + half for dz, dy, half in PIECES])
    pieces, ratio = gradients(target.astype(jnp.int32), toks, outs, ggus, hids)
    ratio = ratio[:, :1]
    factor = jnp.concatenate([ratio] * 3, axis=0)

    def own(k):
        return f32(pieces[k]) * factor

    a, b = to_z(bf(own(0)), 1), to_z(bf(own(1)), -1)
    c, d = to_y_next(bf(own(2))), to_y_next(bf(own(3)))
    e, f = to_z(bf(own(6)), 1), to_z(bf(own(7)), -1)
    g, h = to_z(bf(own(4) + f32(a)), 1), to_z(bf(own(5) + f32(b)), -1)
    left_0, left_1 = to_z(bf(own(8) + f32(e)), 1), to_z(bf(own(9) + f32(c)), 1)
    right_0, right_1 = to_z(bf(own(10) + f32(d)), -1), to_z(bf(own(11) + f32(f)), -1)
    next_0, next_1 = to_y_next(bf(own(12) + f32(g))), to_y_next(bf(own(13) + f32(h)))
    total = ratio + to_y_next(ratio)
    total = total + to_z(total, 2)
    total = total + to_z(total, 1)
    total = jnp.concatenate([total] * 3, axis=0)
    sum_0 = (own(14) + f32(left_0) + f32(right_0) + f32(next_0)) / total
    sum_1 = (own(15) + f32(left_1) + f32(right_1) + f32(next_1)) / total
    weighted = jnp.concatenate([bf(sum_0), bf(sum_1)], axis=1)
    grad_gate = weighted[:hid].T
    grad_up = weighted[hid : 2 * hid].T
    grad_down = weighted[2 * hid :]

    for batch, ggu in zip(BATCHES, ggus):
        size = rows * len(batch)
        block = bf(contract_cols(ggu, both))
        summed = bf(f32(block[:size]) + f32(to_core(block[size:])))
        for i, k in enumerate(batch):
            part[k] = summed[i * rows : (i + 1) * rows]
    far_0, far_1 = to_x(part[6], 1), to_x(part[7], -1)
    up_0 = to_x(bf(f32(part[2]) + f32(far_0)), 1)
    up_1 = to_x(part[5], 1)
    down_0 = to_x(part[1], -1)
    down_1 = to_x(bf(f32(part[4]) + f32(far_1)), -1)
    other = to_y_half(bf(f32(part[3]) + f32(up_1) + f32(down_1)))
    grad_tokens = bf(f32(part[0]) + f32(up_0) + f32(down_0) + f32(other))[None]
    return (grad_tokens, grad_gate, grad_up, grad_down)


def solution(mesh):
    return jax.shard_map(
        body,
        mesh=mesh,
        in_specs=(
            P("lang", "fsdp", None),
            P("lang", "fsdp", None),
            P("lang", None),
            P(None, "fsdp"),
            P(None, "fsdp"),
            P("fsdp", None),
        ),
        out_specs=(
            P("lang", "fsdp", None),
            P("lang", "fsdp"),
            P("lang", "fsdp"),
            P("fsdp", "lang"),
        ),
        check_vma=False,
    )
```

```python
import functools

import jax
import jax.numpy as jnp
from jax import lax
from jax.experimental import pallas as pl
from jax.experimental.pallas import tpu as pltpu
from jax.sharding import PartitionSpec as P


epsilon = 1e-06
INTERPRET = False

PLACES = ((0, 0), (-1, 0), (1, 0), (0, 1), (-1, 1), (1, 1), (2, 0), (2, 1))
BATCHES = ((0, 1, 2, 3), (4, 5, 6), (7,))
PIECES = (
    (2, 1, 0), (2, 1, 1), (1, 1, 1), (-1, 1, 0), (2, 0, 0), (2, 0, 1),
    (1, 1, 0), (-1, 1, 1), (1, 0, 0), (1, 0, 1), (-1, 0, 0), (-1, 0, 1),
    (0, 1, 0), (0, 1, 1), (0, 0, 0), (0, 0, 1),
)
EARLY = 4
ALONE = 2


def fsdp_pairs(dx, dy, dc):
    return [
        (y * 8 + x * 2 + c, (y ^ dy) * 8 + (x + dx) % 4 * 2 + (c ^ dc))
        for y in range(2)
        for x in range(4)
        for c in range(2)
    ]


def lang_pairs(dz, dy):
    return [(z * 2 + y, (z + dz) % 4 * 2 + (y ^ dy)) for z in range(4) for y in range(2)]


def to_x(value, step):
    return lax.ppermute(value, "fsdp", fsdp_pairs(step, 0, 0))


def to_y_half(value):
    return lax.ppermute(value, "fsdp", fsdp_pairs(0, 1, 0))


def to_core(value):
    return lax.ppermute(value, "fsdp", fsdp_pairs(0, 0, 1))


def to_z(value, step):
    return lax.ppermute(value, "lang", lang_pairs(step, 0))


def to_y_next(value):
    return lax.ppermute(value, "lang", lang_pairs(0, 1))


def after(value, *others):
    return lax.optimization_barrier((value, *others))[0]


def forward_kernel(tok, tok_p, out, out_p, wg, wu, wd, inv, ggu_ref, hid_ref, gate, up, back):
    step = pl.program_id(0)
    features = jnp.concatenate([tok[...], tok_p[...]], axis=0)
    upstream = jnp.concatenate([out[...], out_p[...]], axis=0)

    @pl.when(step == 0)
    def _():
        gate[...] = jnp.zeros_like(gate)
        up[...] = jnp.zeros_like(up)
        back[...] = jnp.zeros_like(back)

    gate[...] += jnp.dot(features, wg[...], preferred_element_type=jnp.float32)
    up[...] += jnp.dot(features, wu[...], preferred_element_type=jnp.float32)
    back[...] += lax.dot_general(
        upstream, wd[...], (((1,), (1,)), ((), ())), preferred_element_type=jnp.float32
    )

    @pl.when(step == pl.num_programs(0) - 1)
    def _():
        width = gate.shape[1]
        inverse = inv[...]
        gate_pre = gate[...]
        up_pre = up[...]
        sig = 1.0 / (1.0 + jnp.exp(-gate_pre))
        act = gate_pre * sig
        hid_ref[...] = (act * up_pre * inverse).astype(hid_ref.dtype)
        hid_grad = back[...] * inverse
        gate_grad = hid_grad * up_pre * sig * (1.0 + gate_pre * (1.0 - sig))
        ggu_ref[:, :width] = gate_grad.astype(ggu_ref.dtype)
        ggu_ref[:, width:] = (hid_grad * act).astype(ggu_ref.dtype)


def forward(tok, tok_p, out, out_p, w_gate, w_up, w_down, inverse):
    rows, depth = tok.shape
    hid = w_gate.shape[1]
    block = min(1024, depth)
    act = pl.BlockSpec((rows, block), lambda k: (0, k))
    wide = pl.BlockSpec((block, hid), lambda k: (k, 0))
    return pl.pallas_call(
        forward_kernel,
        name="forward",
        grid=(depth // block,),
        in_specs=[act, act, act, act, wide, wide,
                  pl.BlockSpec((hid, block), lambda k: (0, k)),
                  pl.BlockSpec((2 * rows, 1), lambda k: (0, 0))],
        out_specs=[pl.BlockSpec((2 * rows, 2 * hid), lambda k: (0, 0)),
                   pl.BlockSpec((2 * rows, hid), lambda k: (0, 0))],
        out_shape=[jax.ShapeDtypeStruct((2 * rows, 2 * hid), jnp.bfloat16),
                   jax.ShapeDtypeStruct((2 * rows, hid), jnp.bfloat16)],
        scratch_shapes=[pltpu.VMEM((2 * rows, hid), jnp.float32)] * 3,
        compiler_params=pltpu.CompilerParams(
            dimension_semantics=("arbitrary",), vmem_limit_bytes=24 << 20),
        interpret=INTERPRET,
    )(tok, tok_p, out, out_p, w_gate, w_up, w_down, inverse)


def gradient_step(ggu_t, hid_t, toks, outs, write, moment):
    hid = hid_t.shape[0]
    features = jnp.concatenate([r[...] for r in toks], axis=0)
    upstream = jnp.concatenate([r[...] for r in outs], axis=0)
    first = jnp.dot(ggu_t[...], features, preferred_element_type=jnp.float32)
    second = jnp.dot(hid_t[...], upstream, preferred_element_type=jnp.float32)
    write(jnp.stack([bf(first[:hid]), bf(first[hid:]), bf(second)]))
    lanes = moment.shape[1]
    total = jnp.zeros(moment.shape, jnp.float32)
    for i in range(0, first.shape[1], lanes):
        a = first[:hid, i : i + lanes]
        b = first[hid:, i : i + lanes]
        c = second[:, i : i + lanes]
        total += a * a + b * b + c * c
    moment[...] += total


def to_one(step, alone, rest, value):
    for i, ref in enumerate(alone):
        @pl.when(step == i)
        def _():
            ref[...] = value

    if rest is not None:
        @pl.when(step >= len(alone))
        def _():
            rest[0] = value


def early_kernel(n, place, *refs):
    toks, outs = refs[: 2 * n], refs[2 * n : 4 * n]
    ggus, hids = refs[4 * n : 5 * n], refs[5 * n : 6 * n]
    alone, (ggu_t, hid_t, moment) = refs[6 * n : -3], refs[-3:]
    step = pl.program_id(0)

    @pl.when(step == 0)
    def _():
        ggu = jnp.concatenate([r[...] for r in ggus], axis=0).astype(jnp.float32)
        ggu_t[...] = ggu.T.astype(ggu_t.dtype)
        hidden = jnp.concatenate([r[...] for r in hids], axis=0).astype(jnp.float32)
        hid_t[...] = hidden.T.astype(hid_t.dtype)
        moment[...] = jnp.zeros_like(moment)

    gradient_step(ggu_t, hid_t, toks, outs, functools.partial(to_one, step, alone, None), moment)


def late_kernel(n, depth, place, *refs):
    toks, outs = refs[: 2 * n], refs[2 * n : 4 * n]
    ggu_t, hid_t, begun = refs[4 * n : 4 * n + 3]
    alone, (pieces, ratio, moment) = refs[4 * n + 3 : -3], refs[-3:]
    step = pl.program_id(0)

    @pl.when(step == 0)
    def _():
        moment[...] = begun[...]

    gradient_step(ggu_t, hid_t, toks, outs, functools.partial(to_one, step, alone, pieces), moment)

    @pl.when(step == pl.num_programs(0) - 1)
    def _():
        summed = jnp.sum(moment[...], axis=1, keepdims=True) / (3.0 * depth) + epsilon
        ratio[...] = jnp.broadcast_to(1.0 / summed, ratio.shape)


def same(array):
    zeros = (0,) * array.ndim
    return pl.BlockSpec(array.shape, lambda k, p: zeros)


def gradients_early(place, toks, outs, ggus, hids):
    n = len(ggus)
    depth, hid = toks[0].shape[1], hids[0].shape[1]
    rows = sum(t.shape[0] for t in toks)
    block = depth // len(PIECES)
    acts = [pl.BlockSpec((a.shape[0], block), lambda k, p: (0, p[k])) for a in (*toks, *outs)]
    out_shape = [
        *[jax.ShapeDtypeStruct((3, hid, block), jnp.bfloat16)] * EARLY,
        jax.ShapeDtypeStruct((2 * hid, rows), jnp.bfloat16),
        jax.ShapeDtypeStruct((hid, rows), jnp.bfloat16),
        jax.ShapeDtypeStruct((hid, min(128, block)), jnp.float32),
    ]
    return pl.pallas_call(
        functools.partial(early_kernel, n),
        name="early",
        grid_spec=pltpu.PrefetchScalarGridSpec(
            num_scalar_prefetch=1,
            grid=(EARLY,),
            in_specs=acts + [same(a) for a in (*ggus, *hids)],
            out_specs=[same(a) for a in out_shape],
        ),
        out_shape=out_shape,
        compiler_params=pltpu.CompilerParams(
            dimension_semantics=("arbitrary",), vmem_limit_bytes=24 << 20),
        interpret=INTERPRET,
    )(place, *toks, *outs, *ggus, *hids)


def gradients_late(place, toks, outs, ggu_t, hid_t, moment):
    n = len(toks) // 2
    depth, hid = toks[0].shape[1], hid_t.shape[0]
    block = depth // len(PIECES)
    late = len(PIECES) - EARLY
    alone = [jax.ShapeDtypeStruct((3, hid, block), jnp.bfloat16)] * ALONE
    acts = [pl.BlockSpec((a.shape[0], block), lambda k, p: (0, p[k])) for a in (*toks, *outs)]
    ratio = jax.ShapeDtypeStruct((hid, 128), jnp.float32)
    return pl.pallas_call(
        functools.partial(late_kernel, n, depth),
        name="late",
        grid_spec=pltpu.PrefetchScalarGridSpec(
            num_scalar_prefetch=1,
            grid=(late,),
            in_specs=acts + [same(a) for a in (ggu_t, hid_t, moment)],
            out_specs=[same(a) for a in alone] + [
                pl.BlockSpec((1, 3, hid, block), lambda k, p: (jnp.maximum(k - ALONE, 0), 0, 0, 0)),
                same(ratio)],
            scratch_shapes=[pltpu.VMEM(moment.shape, jnp.float32)],
        ),
        out_shape=alone
        + [jax.ShapeDtypeStruct((late - ALONE, 3, hid, block), jnp.bfloat16), ratio],
        compiler_params=pltpu.CompilerParams(
            dimension_semantics=("arbitrary",), vmem_limit_bytes=24 << 20),
        interpret=INTERPRET,
    )(place, *toks, *outs, ggu_t, hid_t, moment)


def contract_cols(left, right):
    return lax.dot_general(
        left, right, (((1,), (1,)), ((), ())), preferred_element_type=jnp.float32
    )


def bf(value):
    return value.astype(jnp.bfloat16)


def f32(value):
    return value.astype(jnp.float32)


def step(tokens, grad_out, doc_ids, w_gate, w_up, w_down):
    rows = tokens.shape[1]
    lang, fsdp = lax.axis_index("lang"), lax.axis_index("fsdp")
    z, y_lo = lang // 2, lang % 2
    y_hi, x, core = fsdp // 8, fsdp // 2 % 4, fsdp % 2

    t, o = {}, {}
    t[0], o[0] = tokens[0], grad_out[0]
    t[1], t[2], t[3] = to_x(t[0], 1), to_x(t[0], -1), to_y_half(t[0])
    o[1], o[2], o[3] = to_x(o[0], 1), to_x(o[0], -1), to_y_half(o[0])

    segment = doc_ids[0]
    counts = jnp.sum((segment[:, None] == segment[None, :]).astype(jnp.float32), axis=1)
    inverse = (1.0 / counts).reshape(16, rows)
    order = [(k, dc) for batch in BATCHES for dc in (0, 1) for k in batch]
    source = jnp.stack(
        [(y_hi ^ PLACES[k][1]) * 8 + (x + PLACES[k][0]) % 4 * 2 + (core ^ dc) for k, dc in order]
    )
    chosen = source[:, None] == jnp.arange(16)[None, :]
    inverse = jnp.sum(jnp.where(chosen[:, :, None], inverse[None], 0.0), axis=1)
    inverse = inverse.reshape(16 * rows, 1)
    both = jnp.concatenate([w_gate, w_up], axis=1)
    target = jnp.stack([((z + dz) % 4 * 2 + (y_lo ^ dy)) * 2 + half for dz, dy, half in PIECES])
    target = target.astype(jnp.int32)

    t[4], t[5], t[6] = to_y_half(t[1]), to_x(t[3], -1), to_x(t[1], 1)
    o[5], o[4], o[6] = to_y_half(o[2]), to_x(o[3], 1), to_x(o[2], -1)

    toks, outs, ggus, hids = [], [], [], []
    at = 0
    for number, batch in enumerate(BATCHES):
        if number == 1:
            near, t[4], o[5] = input_gradient(ggus[0], both, t[4], o[5])
            t[7], o[7] = to_x(t[4], 1), to_x(o[5], -1)
        size = rows * len(batch)
        tok = jnp.concatenate([t[k] for k in batch], axis=0)
        out = jnp.concatenate([o[k] for k in batch], axis=0)
        tok_p, out_p = to_core(tok), to_core(out)
        ggu, hidden = forward(
            tok, tok_p, out, out_p, w_gate, w_up, w_down, inverse[at : at + 2 * size]
        )
        at += 2 * size
        toks += [tok, tok_p]
        outs += [out, out_p]
        ggus.append(ggu)
        hids.append(hidden)

    *first, ggu_t, hid_t, moment = gradients_early(target[:EARLY], toks, outs, ggus, hids)
    a, b = to_z(first[0], 1), to_z(first[1], -1)
    c, d = to_y_next(first[2]), to_y_next(first[3])
    size = [rows * len(batch) for batch in BATCHES]
    ggu = jnp.concatenate(
        [ggus[1][: size[1]], ggus[2][: size[2]], ggus[1][size[1] :], ggus[2][size[2] :]], axis=0
    )
    far, moment = input_gradient(ggu, both, moment)
    e, f, pieces, ratio = gradients_late(target[EARLY:], toks, outs, ggu_t, hid_t, moment)
    ratio = ratio[:, :1]
    from_low, from_high, from_next = to_z(ratio, 1), to_z(ratio, -1), to_y_next(ratio)

    def own(k):
        return f32(pieces[k - EARLY - ALONE]) * ratio[None]

    def theirs(value, factor):
        return f32(value) * factor[None]

    e, f = to_z(e, 1), to_z(f, -1)
    g = to_z(bf(own(6) + theirs(a, from_low)), 1)
    h = to_z(bf(own(7) + theirs(b, from_high)), -1)
    c, d, e, f = after(c, g, h), after(d, g, h), after(e, g, h), after(f, g, h)
    left_0 = to_z(bf(own(8) + theirs(e, from_low)), 1)
    left_1 = to_z(bf(own(9) + theirs(c, from_next)), 1)
    right_0 = to_z(bf(own(10) + theirs(d, from_next)), -1)
    right_1 = to_z(bf(own(11) + theirs(f, from_high)), -1)
    next_0 = to_y_next(bf(own(12) + f32(g)))
    next_1 = to_y_next(bf(own(13) + f32(h)))
    total = ratio + from_next
    total = total + to_z(total, 2)
    total = total + to_z(total, 1)
    sum_0 = (own(14) + f32(left_0) + f32(right_0) + f32(next_0)) / total[None]
    sum_1 = (own(15) + f32(left_1) + f32(right_1) + f32(next_1)) / total[None]
    weighted = jnp.concatenate([bf(sum_0), bf(sum_1)], axis=2)
    grad_gate, grad_up, grad_down = weighted[0].T, weighted[1].T, weighted[2]

    part = [value[i : i + rows] for value in (near, far) for i in range(0, size[0], rows)]
    far_0, far_1 = to_x(part[6], 1), to_x(part[7], -1)
    up_1 = to_x(part[5], 1)
    down_0 = to_x(part[1], -1)
    up_0 = to_x(bf(f32(part[2]) + f32(far_0)), 1)
    down_1 = to_x(bf(f32(part[4]) + f32(far_1)), -1)
    other = to_y_half(bf(f32(part[3]) + f32(up_1) + f32(down_1)))
    grad_tokens = bf(f32(part[0]) + f32(up_0) + f32(down_0) + f32(other))[None]
    return (grad_tokens, grad_gate, grad_up, grad_down)


def input_gradient(ggu, both, *later):
    size = ggu.shape[0] // 2
    block = bf(contract_cols(ggu, both))
    block, *later = lax.optimization_barrier((block, *later))
    return bf(f32(block[:size]) + f32(to_core(block[size:]))), *later


def solution(mesh):
    return jax.shard_map(
        step,
        mesh=mesh,
        in_specs=(
            P("lang", "fsdp", None),
            P("lang", "fsdp", None),
            P("lang", None),
            P(None, "fsdp"),
            P(None, "fsdp"),
            P("fsdp", None),
        ),
        out_specs=(
            P("lang", "fsdp", None),
            P("lang", "fsdp"),
            P("lang", "fsdp"),
            P("fsdp", "lang"),
        ),
        check_vma=False,
    )
```

```python
import functools

import jax
import jax.numpy as jnp
from jax import lax
from jax.experimental import pallas as pl
from jax.experimental.pallas import tpu as pltpu
from jax.sharding import PartitionSpec as P


epsilon = 1e-06
INTERPRET = False
VMEM = 58 << 20

PLACES = ((0, 0), (-1, 0), (1, 0), (0, 1), (-1, 1), (1, 1), (2, 0), (2, 1))
BATCHES = ((0, 1, 2, 3), (4, 5, 6), (7,))
PIECES = (
    (2, 1, 0), (2, 1, 1), (1, 1, 1), (-1, 1, 0), (2, 0, 0), (2, 0, 1),
    (1, 1, 0), (-1, 1, 1), (1, 0, 0), (1, 0, 1), (-1, 0, 0), (-1, 0, 1),
    (0, 1, 0), (0, 1, 1), (0, 0, 0), (0, 0, 1),
)
EARLY = 4
ALONE = 2


def fsdp_pairs(dx, dy, dc):
    return [
        (y * 8 + x * 2 + c, (y ^ dy) * 8 + (x + dx) % 4 * 2 + (c ^ dc))
        for y in range(2)
        for x in range(4)
        for c in range(2)
    ]


def lang_pairs(dz, dy):
    return [(z * 2 + y, (z + dz) % 4 * 2 + (y ^ dy)) for z in range(4) for y in range(2)]


def to_x(value, step):
    return lax.ppermute(value, "fsdp", fsdp_pairs(step, 0, 0))


def to_y_half(value):
    return lax.ppermute(value, "fsdp", fsdp_pairs(0, 1, 0))


def to_core(value):
    return lax.ppermute(value, "fsdp", fsdp_pairs(0, 0, 1))


def to_z(value, step):
    return lax.ppermute(value, "lang", lang_pairs(step, 0))


def to_y_next(value):
    return lax.ppermute(value, "lang", lang_pairs(0, 1))


def after(value, *others):
    return lax.optimization_barrier((value, *others))[0]


def forward_kernel(n, *refs):
    toks, outs = refs[:n], refs[n : 2 * n]
    wg, wu, wd, inv, ggu_ref, hid_ref, gate, up, back = refs[2 * n :]
    step = pl.program_id(0)
    features = jnp.concatenate([r[...] for r in toks], axis=0)
    upstream = jnp.concatenate([r[...] for r in outs], axis=0)

    @pl.when(step == 0)
    def _():
        gate[...] = jnp.zeros_like(gate)
        up[...] = jnp.zeros_like(up)
        back[...] = jnp.zeros_like(back)

    gate[...] += jnp.dot(features, wg[...], preferred_element_type=jnp.float32)
    up[...] += jnp.dot(features, wu[...], preferred_element_type=jnp.float32)
    back[...] += contract_cols(upstream, wd[...])

    @pl.when(step == pl.num_programs(0) - 1)
    def _():
        width = gate.shape[1]
        inverse = inv[...]
        gate_pre = gate[...]
        up_pre = up[...]
        sig = 1.0 / (1.0 + jnp.exp(-gate_pre))
        act = gate_pre * sig
        hid_ref[...] = (act * up_pre * inverse).astype(hid_ref.dtype)
        hid_grad = back[...] * inverse
        gate_grad = hid_grad * up_pre * sig * (1.0 + gate_pre * (1.0 - sig))
        ggu_ref[:, :width] = gate_grad.astype(ggu_ref.dtype)
        ggu_ref[:, width:] = (hid_grad * act).astype(ggu_ref.dtype)


def forward(toks, outs, w_gate, w_up, w_down, inverse):
    n = len(toks)
    rows, depth = toks[0].shape
    hid = w_gate.shape[1]
    block = min(1024, depth)
    act = pl.BlockSpec((rows, block), lambda k: (0, k))
    wide = pl.BlockSpec((block, hid), lambda k: (k, 0))
    return pl.pallas_call(
        functools.partial(forward_kernel, n),
        name="forward",
        grid=(depth // block,),
        in_specs=[act] * (2 * n) + [wide, wide,
                  pl.BlockSpec((hid, block), lambda k: (0, k)),
                  pl.BlockSpec((n * rows, 1), lambda k: (0, 0))],
        out_specs=[pl.BlockSpec((n * rows, 2 * hid), lambda k: (0, 0)),
                   pl.BlockSpec((n * rows, hid), lambda k: (0, 0))],
        out_shape=[jax.ShapeDtypeStruct((n * rows, 2 * hid), jnp.bfloat16),
                   jax.ShapeDtypeStruct((n * rows, hid), jnp.bfloat16)],
        scratch_shapes=[pltpu.VMEM((n * rows, hid), jnp.float32)] * 3,
        compiler_params=pltpu.CompilerParams(
            dimension_semantics=("arbitrary",), vmem_limit_bytes=VMEM),
        interpret=INTERPRET,
    )(*toks, *outs, w_gate, w_up, w_down, inverse)


def input_kernel(n, *refs):
    ggus, (wg, wu, own, theirs) = refs[:n], refs[n:]
    hid = wg.shape[1]
    half = [r.shape[0] // 2 for r in ggus]
    ggu = jnp.concatenate(
        [r[:h] for r, h in zip(ggus, half)] + [r[h:] for r, h in zip(ggus, half)], axis=0
    )
    total = contract_cols(ggu[:, :hid], wg[...]) + contract_cols(ggu[:, hid:], wu[...])
    size = own.shape[0]
    own[...] = bf(total[:size])
    theirs[...] = bf(total[size:])


def input_gradient(ggus, w_gate, w_up):
    depth, hid = w_gate.shape
    block = min(1024, depth)
    size = sum(g.shape[0] for g in ggus) // 2
    wide = pl.BlockSpec((block, hid), lambda k: (k, 0))
    return pl.pallas_call(
        functools.partial(input_kernel, len(ggus)),
        name="input",
        grid=(depth // block,),
        in_specs=[pl.BlockSpec(g.shape, lambda k: (0, 0)) for g in ggus] + [wide, wide],
        out_specs=[pl.BlockSpec((size, block), lambda k: (0, k))] * 2,
        out_shape=[jax.ShapeDtypeStruct((size, depth), jnp.bfloat16)] * 2,
        compiler_params=pltpu.CompilerParams(
            dimension_semantics=("arbitrary",), vmem_limit_bytes=VMEM),
        interpret=INTERPRET,
    )(*ggus, w_gate, w_up)


def last_kernel(pieces, l0, l1, r0, r1, n0, n1, ratio, total, gate, up, down):
    block = pieces.shape[3]
    factor, divisor = ratio[...], total[...]
    for half, group in enumerate(((l0, r0, n0), (l1, r1, n1))):
        at = half * block
        for m, ref in enumerate((gate, up, down)):
            value = f32(pieces[half, m]) * factor
            for other in group:
                value += f32(other[m])
            value = value / divisor
            if m == 2:
                ref[:, at : at + block] = bf(value)
            else:
                ref[at : at + block, :] = bf(value.T)


def last_sum(pieces, others, ratio, total):
    count, _, hid, block = pieces.shape
    whole = [pl.BlockSpec(a.shape, lambda k, n=a.ndim: (0,) * n) for a in (*others, ratio, total)]
    shapes = [(2 * block, hid), (2 * block, hid), (hid, 2 * block)]
    return pl.pallas_call(
        last_kernel,
        name="last",
        grid=(1,),
        in_specs=[pl.BlockSpec((2, 3, hid, block), lambda k: (count // 2 - 1, 0, 0, 0))] + whole,
        out_specs=[pl.BlockSpec(shape, lambda k: (0, 0)) for shape in shapes],
        out_shape=[jax.ShapeDtypeStruct(shape, jnp.bfloat16) for shape in shapes],
        compiler_params=pltpu.CompilerParams(vmem_limit_bytes=VMEM),
        interpret=INTERPRET,
    )(pieces, *others, ratio, total)


def gradient_step(ggu_t, hid_t, toks, outs, write, moment):
    hid = hid_t.shape[0]
    features = jnp.concatenate([r[...] for r in toks], axis=0)
    upstream = jnp.concatenate([r[...] for r in outs], axis=0)
    first = jnp.dot(ggu_t[...], features, preferred_element_type=jnp.float32)
    second = jnp.dot(hid_t[...], upstream, preferred_element_type=jnp.float32)
    write(jnp.stack([bf(first[:hid]), bf(first[hid:]), bf(second)]))
    lanes = moment.shape[1]
    total = jnp.zeros(moment.shape, jnp.float32)
    for i in range(0, first.shape[1], lanes):
        a = first[:hid, i : i + lanes]
        b = first[hid:, i : i + lanes]
        c = second[:, i : i + lanes]
        total += a * a + b * b + c * c
    moment[...] += total


def to_one(step, alone, rest, value):
    for i, ref in enumerate(alone):
        @pl.when(step == i)
        def _():
            ref[...] = value

    if rest is not None:
        @pl.when(step >= len(alone))
        def _():
            rest[0] = value


def early_kernel(m, n, place, *refs):
    toks, outs = refs[:m], refs[m : 2 * m]
    ggus, hids = refs[2 * m : 2 * m + n], refs[2 * m + n : 2 * m + 2 * n]
    alone, (ggu_t, hid_t, moment) = refs[2 * m + 2 * n : -3], refs[-3:]
    step = pl.program_id(0)

    @pl.when(step == 0)
    def _():
        ggu = jnp.concatenate([r[...] for r in ggus], axis=0).astype(jnp.float32)
        ggu_t[...] = ggu.T.astype(ggu_t.dtype)
        hidden = jnp.concatenate([r[...] for r in hids], axis=0).astype(jnp.float32)
        hid_t[...] = hidden.T.astype(hid_t.dtype)
        moment[...] = jnp.zeros_like(moment)

    gradient_step(ggu_t, hid_t, toks, outs, functools.partial(to_one, step, alone, None), moment)


def late_kernel(m, depth, place, *refs):
    toks, outs = refs[:m], refs[m : 2 * m]
    ggu_t, hid_t, begun = refs[2 * m : 2 * m + 3]
    alone, (pieces, ratio, moment) = refs[2 * m + 3 : -3], refs[-3:]
    step = pl.program_id(0)

    @pl.when(step == 0)
    def _():
        moment[...] = begun[...]

    gradient_step(ggu_t, hid_t, toks, outs, functools.partial(to_one, step, alone, pieces), moment)

    @pl.when(step == pl.num_programs(0) - 1)
    def _():
        summed = jnp.sum(moment[...], axis=1, keepdims=True) / (3.0 * depth) + epsilon
        ratio[...] = jnp.broadcast_to(1.0 / summed, ratio.shape)


def same(array):
    zeros = (0,) * array.ndim
    return pl.BlockSpec(array.shape, lambda k, p: zeros)


def gradients_early(place, toks, outs, ggus, hids):
    n = len(ggus)
    depth, hid = toks[0].shape[1], hids[0].shape[1]
    rows = sum(t.shape[0] for t in toks)
    block = depth // len(PIECES)
    acts = [pl.BlockSpec((a.shape[0], block), lambda k, p: (0, p[k])) for a in (*toks, *outs)]
    out_shape = [
        *[jax.ShapeDtypeStruct((3, hid, block), jnp.bfloat16)] * EARLY,
        jax.ShapeDtypeStruct((2 * hid, rows), jnp.bfloat16),
        jax.ShapeDtypeStruct((hid, rows), jnp.bfloat16),
        jax.ShapeDtypeStruct((hid, min(128, block)), jnp.float32),
    ]
    return pl.pallas_call(
        functools.partial(early_kernel, len(toks), n),
        name="early",
        grid_spec=pltpu.PrefetchScalarGridSpec(
            num_scalar_prefetch=1,
            grid=(EARLY,),
            in_specs=acts + [same(a) for a in (*ggus, *hids)],
            out_specs=[same(a) for a in out_shape],
        ),
        out_shape=out_shape,
        compiler_params=pltpu.CompilerParams(
            dimension_semantics=("arbitrary",), vmem_limit_bytes=VMEM),
        interpret=INTERPRET,
    )(place, *toks, *outs, *ggus, *hids)


def gradients_late(place, toks, outs, ggu_t, hid_t, moment):
    depth, hid = toks[0].shape[1], hid_t.shape[0]
    block = depth // len(PIECES)
    late = len(PIECES) - EARLY
    alone = [jax.ShapeDtypeStruct((3, hid, block), jnp.bfloat16)] * ALONE
    acts = [pl.BlockSpec((a.shape[0], block), lambda k, p: (0, p[k])) for a in (*toks, *outs)]
    ratio = jax.ShapeDtypeStruct((hid, 128), jnp.float32)
    return pl.pallas_call(
        functools.partial(late_kernel, len(toks), depth),
        name="late",
        grid_spec=pltpu.PrefetchScalarGridSpec(
            num_scalar_prefetch=1,
            grid=(late,),
            in_specs=acts + [same(a) for a in (ggu_t, hid_t, moment)],
            out_specs=[same(a) for a in alone] + [
                pl.BlockSpec((1, 3, hid, block), lambda k, p: (jnp.maximum(k - ALONE, 0), 0, 0, 0)),
                same(ratio)],
            scratch_shapes=[pltpu.VMEM(moment.shape, jnp.float32)],
        ),
        out_shape=alone
        + [jax.ShapeDtypeStruct((late - ALONE, 3, hid, block), jnp.bfloat16), ratio],
        compiler_params=pltpu.CompilerParams(
            dimension_semantics=("arbitrary",), vmem_limit_bytes=VMEM),
        interpret=INTERPRET,
    )(place, *toks, *outs, ggu_t, hid_t, moment)


def contract_cols(left, right):
    return lax.dot_general(
        left, right, (((1,), (1,)), ((), ())), preferred_element_type=jnp.float32
    )


def bf(value):
    return value.astype(jnp.bfloat16)


def f32(value):
    return value.astype(jnp.float32)


def step(tokens, grad_out, doc_ids, w_gate, w_up, w_down):
    rows = tokens.shape[1]
    lang, fsdp = lax.axis_index("lang"), lax.axis_index("fsdp")
    z, y_lo = lang // 2, lang % 2
    y_hi, x, core = fsdp // 8, fsdp // 2 % 4, fsdp % 2

    t, o = {}, {}
    t[0], o[0] = tokens[0], grad_out[0]
    t[1], t[2], t[3] = to_x(t[0], 1), to_x(t[0], -1), to_y_half(t[0])
    o[1], o[2], o[3] = to_x(o[0], 1), to_x(o[0], -1), to_y_half(o[0])

    segment = doc_ids[0]
    same_document = (segment[:, None] == segment[None, :]).astype(jnp.float32)
    inverse = (1.0 / jnp.sum(same_document, axis=1)).reshape(16, rows)
    order = [(k, dc) for batch in BATCHES for dc in (0, 1) for k in batch]
    source = jnp.stack(
        [(y_hi ^ PLACES[k][1]) * 8 + (x + PLACES[k][0]) % 4 * 2 + (core ^ dc) for k, dc in order]
    )
    chosen = source[:, None] == jnp.arange(16)[None, :]
    inverse = jnp.sum(jnp.where(chosen[:, :, None], inverse[None], 0.0), axis=1)
    inverse = inverse.reshape(16 * rows, 1)
    target = jnp.stack([((z + dz) % 4 * 2 + (y_lo ^ dy)) * 2 + half for dz, dy, half in PIECES])
    target = target.astype(jnp.int32)

    t[4], t[5], t[6] = to_y_half(t[1]), to_x(t[3], -1), to_x(t[1], 1)
    o[5], o[4], o[6] = to_y_half(o[2]), to_x(o[3], 1), to_x(o[2], -1)

    t[7], o[7] = to_x(t[4], 1), to_x(o[5], -1)

    toks, outs, ggus, hids = [], [], [], []
    at = 0
    for batch in BATCHES:
        tok, out = [t[k] for k in batch], [o[k] for k in batch]
        tok += [to_core(v) for v in tok]
        out += [to_core(v) for v in out]
        size = rows * len(tok)
        ggu, hidden = forward(tok, out, w_gate, w_up, w_down, inverse[at : at + size])
        at += size
        toks += tok
        outs += out
        ggus.append(ggu)
        hids.append(hidden)
    near, near_p = input_gradient(ggus[:1], w_gate, w_up)
    near = bf(f32(near) + f32(to_core(near_p)))

    *first, ggu_t, hid_t, moment = gradients_early(target[:EARLY], toks, outs, ggus, hids)
    a, b = to_z(first[0], 1), to_z(first[1], -1)
    c, d = to_y_next(first[2]), to_y_next(first[3])
    far, far_p = input_gradient([after(ggus[1], moment), ggus[2]], w_gate, w_up)
    far_p, moment = lax.optimization_barrier((far_p, moment))
    far = bf(f32(far) + f32(to_core(far_p)))
    e, f, pieces, ratio = gradients_late(target[EARLY:], toks, outs, ggu_t, hid_t, moment)
    ratio = ratio[:, :1]
    from_low, from_high, from_next = to_z(ratio, 1), to_z(ratio, -1), to_y_next(ratio)

    def own(k):
        return f32(pieces[k - EARLY - ALONE]) * ratio[None]

    def theirs(value, factor):
        return f32(value) * factor[None]

    e, f = to_z(e, 1), to_z(f, -1)
    g = to_z(bf(own(6) + theirs(a, from_low)), 1)
    h = to_z(bf(own(7) + theirs(b, from_high)), -1)
    from_next = after(from_next, g, h)
    c, d, e, f = after(c, g, h), after(d, g, h), after(e, g, h), after(f, g, h)
    left_0 = to_z(bf(own(8) + theirs(e, from_low)), 1)
    left_1 = to_z(bf(own(9) + theirs(c, from_next)), 1)
    right_0 = to_z(bf(own(10) + theirs(d, from_next)), -1)
    right_1 = to_z(bf(own(11) + theirs(f, from_high)), -1)
    next_0 = to_y_next(bf(own(12) + f32(g)))
    next_1 = to_y_next(bf(own(13) + f32(h)))
    total = ratio + from_next
    total = total + to_z(total, 2)
    total = total + to_z(total, 1)
    others = (left_0, left_1, right_0, right_1, next_0, next_1)
    grad_gate, grad_up, grad_down = last_sum(pieces, others, ratio, total)

    part = [value[i : i + rows] for value in (near, far) for i in range(0, 4 * rows, rows)]
    far_0, far_1 = to_x(part[6], 1), to_x(part[7], -1)
    up_1, down_0 = to_x(part[5], 1), to_x(part[1], -1)
    up_0, down_1 = bf(f32(part[2]) + f32(far_0)), bf(f32(part[4]) + f32(far_1))
    up_0, down_1 = to_x(up_0, 1), to_x(down_1, -1)
    other = bf(f32(part[3]) + f32(up_1) + f32(down_1))
    other = to_y_half(other)
    grad_tokens = bf(f32(part[0]) + f32(up_0) + f32(down_0) + f32(other))[None]
    return (grad_tokens, grad_gate, grad_up, grad_down)


def solution(mesh):
    return jax.shard_map(
        step,
        mesh=mesh,
        in_specs=(
            P("lang", "fsdp", None),
            P("lang", "fsdp", None),
            P("lang", None),
            P(None, "fsdp"),
            P(None, "fsdp"),
            P("fsdp", None),
        ),
        out_specs=(
            P("lang", "fsdp", None),
            P("lang", "fsdp"),
            P("lang", "fsdp"),
            P("fsdp", "lang"),
        ),
        check_vma=False,
    )
```

```python
import functools

import jax
import jax.numpy as jnp
from jax import lax
from jax.experimental import pallas as pl
from jax.experimental.pallas import tpu as pltpu
from jax.sharding import PartitionSpec as P


epsilon = 1e-06
INTERPRET = False
VMEM = (64 << 20) - 400000
VMEM_SMALL = 20 << 20

PLACES = ((0, 0), (-1, 0), (1, 0), (0, 1), (-1, 1), (1, 1), (2, 0), (2, 1))
BATCHES = ((0, 1, 2, 3), (4, 5, 6), (7,))
PIECES = (
    (2, 1, 0), (2, 1, 1), (1, 1, 1), (-1, 1, 0), (2, 0, 0), (2, 0, 1),
    (1, 1, 0), (-1, 1, 1), (1, 0, 0), (1, 0, 1), (-1, 0, 0), (-1, 0, 1),
    (0, 1, 0), (0, 1, 1), (0, 0, 0), (0, 0, 1),
)
EARLY = 4
ALONE = 2


def fsdp_pairs(dx, dy, dc):
    return [
        (y * 8 + x * 2 + c, (y ^ dy) * 8 + (x + dx) % 4 * 2 + (c ^ dc))
        for y in range(2)
        for x in range(4)
        for c in range(2)
    ]


def lang_pairs(dz, dy):
    return [(z * 2 + y, (z + dz) % 4 * 2 + (y ^ dy)) for z in range(4) for y in range(2)]


def to_x(value, step):
    return lax.ppermute(value, "fsdp", fsdp_pairs(step, 0, 0))


def to_y_half(value):
    return lax.ppermute(value, "fsdp", fsdp_pairs(0, 1, 0))


def to_core(value):
    return lax.ppermute(value, "fsdp", fsdp_pairs(0, 0, 1))


def to_z(value, step):
    return lax.ppermute(value, "lang", lang_pairs(step, 0))


def to_y_next(value):
    return lax.ppermute(value, "lang", lang_pairs(0, 1))


def after(value, *others):
    return lax.optimization_barrier((value, *others))[0]


def forward_kernel(n, *refs):
    toks, outs = refs[:n], refs[n : 2 * n]
    wg, wu, wd, inv, ggu_ref, hid_ref, tok_ref, out_ref, gate, up, back = refs[2 * n :]
    step = pl.program_id(0)
    features = jnp.concatenate([r[...] for r in toks], axis=0)
    upstream = jnp.concatenate([r[...] for r in outs], axis=0)
    tok_ref[...] = features
    out_ref[...] = upstream

    @pl.when(step == 0)
    def _():
        gate[...] = jnp.zeros_like(gate)
        up[...] = jnp.zeros_like(up)
        back[...] = jnp.zeros_like(back)

    gate[...] += jnp.dot(features, wg[...], preferred_element_type=jnp.float32)
    up[...] += jnp.dot(features, wu[...], preferred_element_type=jnp.float32)
    back[...] += contract_cols(upstream, wd[...])

    @pl.when(step == pl.num_programs(0) - 1)
    def _():
        width = gate.shape[1]
        inverse = inv[...]
        gate_pre = gate[...]
        up_pre = up[...]
        sig = 1.0 / (1.0 + jnp.exp(-gate_pre))
        act = gate_pre * sig
        hid_ref[...] = (act * up_pre * inverse).astype(hid_ref.dtype)
        hid_grad = back[...] * inverse
        gate_grad = hid_grad * up_pre * sig * (1.0 + gate_pre * (1.0 - sig))
        ggu_ref[:, :width] = gate_grad.astype(ggu_ref.dtype)
        ggu_ref[:, width:] = (hid_grad * act).astype(ggu_ref.dtype)


def forward(toks, outs, w_gate, w_up, w_down, inverse):
    n = len(toks)
    rows, depth = toks[0].shape
    hid = w_gate.shape[1]
    block = min(1024, depth)
    act = pl.BlockSpec((rows, block), lambda k: (0, k))
    wide = pl.BlockSpec((block, hid), lambda k: (k, 0))
    return pl.pallas_call(
        functools.partial(forward_kernel, n),
        name="forward",
        grid=(depth // block,),
        in_specs=[act] * (2 * n) + [wide, wide,
                  pl.BlockSpec((hid, block), lambda k: (0, k)),
                  pl.BlockSpec((n * rows, 1), lambda k: (0, 0))],
        out_specs=[pl.BlockSpec((n * rows, 2 * hid), lambda k: (0, 0)),
                   pl.BlockSpec((n * rows, hid), lambda k: (0, 0))]
        + [pl.BlockSpec((n * rows, block), lambda k: (0, k))] * 2,
        out_shape=[jax.ShapeDtypeStruct((n * rows, 2 * hid), jnp.bfloat16),
                   jax.ShapeDtypeStruct((n * rows, hid), jnp.bfloat16)]
        + [jax.ShapeDtypeStruct((n * rows, depth), jnp.bfloat16)] * 2,
        scratch_shapes=[pltpu.VMEM((n * rows, hid), jnp.float32)] * 3,
        compiler_params=pltpu.CompilerParams(
            dimension_semantics=("arbitrary",), vmem_limit_bytes=VMEM),
        interpret=INTERPRET,
    )(*toks, *outs, w_gate, w_up, w_down, inverse)


def input_kernel(n, *refs):
    ggus, (wg, wu, own, theirs) = refs[:n], refs[n:]
    hid = wg.shape[1]
    half = [r.shape[0] // 2 for r in ggus]
    ggu = jnp.concatenate(
        [r[:h] for r, h in zip(ggus, half)] + [r[h:] for r, h in zip(ggus, half)], axis=0
    )
    total = contract_cols(ggu[:, :hid], wg[...]) + contract_cols(ggu[:, hid:], wu[...])
    size = own.shape[0]
    own[...] = bf(total[:size])
    theirs[...] = bf(total[size:])


def input_gradient(ggus, w_gate, w_up):
    depth, hid = w_gate.shape
    block = min(1024, depth)
    size = sum(g.shape[0] for g in ggus) // 2
    wide = pl.BlockSpec((block, hid), lambda k: (k, 0))
    return pl.pallas_call(
        functools.partial(input_kernel, len(ggus)),
        name="input",
        grid=(depth // block,),
        in_specs=[pl.BlockSpec(g.shape, lambda k: (0, 0)) for g in ggus] + [wide, wide],
        out_specs=[pl.BlockSpec((size, block), lambda k: (0, k))] * 2,
        out_shape=[jax.ShapeDtypeStruct((size, depth), jnp.bfloat16)] * 2,
        compiler_params=pltpu.CompilerParams(
            dimension_semantics=("arbitrary",), vmem_limit_bytes=VMEM),
        interpret=INTERPRET,
    )(*ggus, w_gate, w_up)


def relay_kernel(pieces, a, b, ratio, low, high, left, right):
    factor = ratio[:, :1]
    for half, (value, other, out) in enumerate(((a, low, left), (b, high, right))):
        scale = other[:, :1]
        for m in range(3):
            out[m] = bf(f32(pieces[half, m]) * factor + f32(value[m]) * scale)


def relay(pieces, a, b, ratio, low, high):
    _, _, hid, block = pieces.shape
    whole = [pl.BlockSpec(v.shape, lambda k, n=v.ndim: (0,) * n) for v in (a, b, ratio, low, high)]
    return pl.pallas_call(
        relay_kernel,
        name="relay",
        grid=(1,),
        in_specs=[pl.BlockSpec((2, 3, hid, block), lambda k: (0, 0, 0, 0))] + whole,
        out_specs=whole[:2],
        out_shape=[jax.ShapeDtypeStruct(a.shape, jnp.bfloat16)] * 2,
        compiler_params=pltpu.CompilerParams(vmem_limit_bytes=VMEM_SMALL),
        interpret=INTERPRET,
    )(pieces, a, b, ratio, low, high)


def last_kernel(pieces, l0, l1, r0, r1, n0, n1, ratio, total, gate, up, down):
    block = pieces.shape[3]
    factor, divisor = ratio[...], total[...]
    for half, group in enumerate(((l0, r0, n0), (l1, r1, n1))):
        at = half * block
        for m, ref in enumerate((gate, up, down)):
            value = f32(pieces[half, m]) * factor
            for other in group:
                value += f32(other[m])
            value = value / divisor
            if m == 2:
                ref[:, at : at + block] = bf(value)
            else:
                ref[at : at + block, :] = bf(value.T)


def last_sum(pieces, others, ratio, total):
    count, _, hid, block = pieces.shape
    whole = [pl.BlockSpec(a.shape, lambda k, n=a.ndim: (0,) * n) for a in (*others, ratio, total)]
    shapes = [(2 * block, hid), (2 * block, hid), (hid, 2 * block)]
    return pl.pallas_call(
        last_kernel,
        name="last",
        grid=(1,),
        in_specs=[pl.BlockSpec((2, 3, hid, block), lambda k: (count // 2 - 1, 0, 0, 0))] + whole,
        out_specs=[pl.BlockSpec(shape, lambda k: (0, 0)) for shape in shapes],
        out_shape=[jax.ShapeDtypeStruct(shape, jnp.bfloat16) for shape in shapes],
        compiler_params=pltpu.CompilerParams(vmem_limit_bytes=VMEM_SMALL),
        interpret=INTERPRET,
    )(pieces, *others, ratio, total)


def gradient_step(ggu_t, hid_t, toks, outs, write, moment):
    hid = hid_t.shape[0]
    features = jnp.concatenate([r[...] for r in toks], axis=0)
    upstream = jnp.concatenate([r[...] for r in outs], axis=0)
    first = jnp.dot(ggu_t[...], features, preferred_element_type=jnp.float32)
    second = jnp.dot(hid_t[...], upstream, preferred_element_type=jnp.float32)
    write(jnp.stack([bf(first[:hid]), bf(first[hid:]), bf(second)]))
    lanes = moment.shape[1]
    total = jnp.zeros(moment.shape, jnp.float32)
    for i in range(0, first.shape[1], lanes):
        a = first[:hid, i : i + lanes]
        b = first[hid:, i : i + lanes]
        c = second[:, i : i + lanes]
        total += a * a + b * b + c * c
    moment[...] += total


def to_one(step, alone, rest, value):
    for i, ref in enumerate(alone):
        @pl.when(step == i)
        def _():
            ref[...] = value

    if rest is not None:
        @pl.when(step >= len(alone))
        def _():
            rest[0] = value


def early_kernel(m, n, place, *refs):
    toks, outs = refs[:m], refs[m : 2 * m]
    ggus, hids = refs[2 * m : 2 * m + n], refs[2 * m + n : 2 * m + 2 * n]
    alone, (ggu_t, hid_t, moment) = refs[2 * m + 2 * n : -3], refs[-3:]
    step = pl.program_id(0)

    @pl.when(step == 0)
    def _():
        ggu = jnp.concatenate([r[...] for r in ggus], axis=0).astype(jnp.float32)
        ggu_t[...] = ggu.T.astype(ggu_t.dtype)
        hidden = jnp.concatenate([r[...] for r in hids], axis=0).astype(jnp.float32)
        hid_t[...] = hidden.T.astype(hid_t.dtype)
        moment[...] = jnp.zeros_like(moment)

    gradient_step(ggu_t, hid_t, toks, outs, functools.partial(to_one, step, alone, None), moment)


def late_kernel(m, depth, place, *refs):
    toks, outs = refs[:m], refs[m : 2 * m]
    ggu_t, hid_t, begun = refs[2 * m : 2 * m + 3]
    alone, (pieces, ratio, moment) = refs[2 * m + 3 : -3], refs[-3:]
    step = pl.program_id(0)

    @pl.when(step == 0)
    def _():
        moment[...] = begun[...]

    gradient_step(ggu_t, hid_t, toks, outs, functools.partial(to_one, step, alone, pieces), moment)

    @pl.when(step == pl.num_programs(0) - 1)
    def _():
        summed = jnp.sum(moment[...], axis=1, keepdims=True) / (3.0 * depth) + epsilon
        ratio[...] = jnp.broadcast_to(1.0 / summed, ratio.shape)


def same(array):
    zeros = (0,) * array.ndim
    return pl.BlockSpec(array.shape, lambda k, p: zeros)


def gradients_early(place, toks, outs, ggus, hids):
    n = len(ggus)
    depth, hid = toks[0].shape[1], hids[0].shape[1]
    rows = sum(t.shape[0] for t in toks)
    block = depth // len(PIECES)
    acts = [pl.BlockSpec((a.shape[0], block), lambda k, p: (0, p[k])) for a in (*toks, *outs)]
    out_shape = [
        *[jax.ShapeDtypeStruct((3, hid, block), jnp.bfloat16)] * EARLY,
        jax.ShapeDtypeStruct((2 * hid, rows), jnp.bfloat16),
        jax.ShapeDtypeStruct((hid, rows), jnp.bfloat16),
        jax.ShapeDtypeStruct((hid, min(128, block)), jnp.float32),
    ]
    return pl.pallas_call(
        functools.partial(early_kernel, len(toks), n),
        name="early",
        grid_spec=pltpu.PrefetchScalarGridSpec(
            num_scalar_prefetch=1,
            grid=(EARLY,),
            in_specs=acts + [same(a) for a in (*ggus, *hids)],
            out_specs=[same(a) for a in out_shape],
        ),
        out_shape=out_shape,
        compiler_params=pltpu.CompilerParams(
            dimension_semantics=("arbitrary",), vmem_limit_bytes=VMEM),
        interpret=INTERPRET,
    )(place, *toks, *outs, *ggus, *hids)


def gradients_late(place, toks, outs, ggu_t, hid_t, moment):
    depth, hid = toks[0].shape[1], hid_t.shape[0]
    block = depth // len(PIECES)
    late = len(PIECES) - EARLY
    alone = [jax.ShapeDtypeStruct((3, hid, block), jnp.bfloat16)] * ALONE
    acts = [pl.BlockSpec((a.shape[0], block), lambda k, p: (0, p[k])) for a in (*toks, *outs)]
    ratio = jax.ShapeDtypeStruct((hid, 128), jnp.float32)
    return pl.pallas_call(
        functools.partial(late_kernel, len(toks), depth),
        name="late",
        grid_spec=pltpu.PrefetchScalarGridSpec(
            num_scalar_prefetch=1,
            grid=(late,),
            in_specs=acts + [same(a) for a in (ggu_t, hid_t, moment)],
            out_specs=[same(a) for a in alone] + [
                pl.BlockSpec((1, 3, hid, block), lambda k, p: (jnp.maximum(k - ALONE, 0), 0, 0, 0)),
                same(ratio)],
            scratch_shapes=[pltpu.VMEM(moment.shape, jnp.float32)],
        ),
        out_shape=alone
        + [jax.ShapeDtypeStruct((late - ALONE, 3, hid, block), jnp.bfloat16), ratio],
        compiler_params=pltpu.CompilerParams(
            dimension_semantics=("arbitrary",), vmem_limit_bytes=VMEM),
        interpret=INTERPRET,
    )(place, *toks, *outs, ggu_t, hid_t, moment)


def contract_cols(left, right):
    return lax.dot_general(
        left, right, (((1,), (1,)), ((), ())), preferred_element_type=jnp.float32
    )


def bf(value):
    return value.astype(jnp.bfloat16)


def f32(value):
    return value.astype(jnp.float32)


def step(tokens, grad_out, doc_ids, w_gate, w_up, w_down):
    rows = tokens.shape[1]
    lang, fsdp = lax.axis_index("lang"), lax.axis_index("fsdp")
    z, y_lo = lang // 2, lang % 2
    y_hi, x, core = fsdp // 8, fsdp // 2 % 4, fsdp % 2

    t, o = {}, {}
    t[0], o[0] = tokens[0], grad_out[0]
    t[1], t[2], t[3] = to_x(t[0], 1), to_x(t[0], -1), to_y_half(t[0])
    o[1], o[2], o[3] = to_x(o[0], 1), to_x(o[0], -1), to_y_half(o[0])

    segment = doc_ids[0]
    same_document = (segment[:, None] == segment[None, :]).astype(jnp.float32)
    inverse = (1.0 / jnp.sum(same_document, axis=1)).reshape(16, rows)
    order = [(k, dc) for batch in BATCHES for dc in (0, 1) for k in batch]
    source = jnp.stack(
        [(y_hi ^ PLACES[k][1]) * 8 + (x + PLACES[k][0]) % 4 * 2 + (core ^ dc) for k, dc in order]
    )
    chosen = source[:, None] == jnp.arange(16)[None, :]
    inverse = jnp.sum(jnp.where(chosen[:, :, None], inverse[None], 0.0), axis=1)
    inverse = inverse.reshape(16 * rows, 1)
    target = jnp.stack([((z + dz) % 4 * 2 + (y_lo ^ dy)) * 2 + half for dz, dy, half in PIECES])
    target = target.astype(jnp.int32)

    t[4], t[5], t[6] = to_y_half(t[1]), to_x(t[3], -1), to_x(t[1], 1)
    o[5], o[4], o[6] = to_y_half(o[2]), to_x(o[3], 1), to_x(o[2], -1)

    t[7], o[7] = to_x(t[4], 1), to_x(o[5], -1)

    toks, outs, ggus, hids = [], [], [], []
    at = 0
    for batch in BATCHES:
        tok, out = [t[k] for k in batch], [o[k] for k in batch]
        tok += [to_core(v) for v in tok]
        out += [to_core(v) for v in out]
        size = rows * len(tok)
        ggu, hidden, tok, out = forward(
            tok, out, w_gate, w_up, w_down, inverse[at : at + size])
        at += size
        toks.append(tok)
        outs.append(out)
        ggus.append(ggu)
        hids.append(hidden)
    near, near_p = input_gradient(ggus[:1], w_gate, w_up)
    near = bf(f32(near) + f32(to_core(near_p)))

    *first, ggu_t, hid_t, moment = gradients_early(target[:EARLY], toks, outs, ggus, hids)
    a, b = to_z(first[0], 1), to_z(first[1], -1)
    c, d = to_y_next(first[2]), to_y_next(first[3])
    far, far_p = input_gradient([after(ggus[1], moment), ggus[2]], w_gate, w_up)
    far_p, moment = lax.optimization_barrier((far_p, moment))
    far = bf(f32(far) + f32(to_core(far_p)))
    e, f, pieces, ratio = gradients_late(target[EARLY:], toks, outs, ggu_t, hid_t, moment)
    low, high = to_z(ratio, 1), to_z(ratio, -1)
    left, right = relay(pieces, a, b, ratio, low, high)
    ratio = ratio[:, :1]
    from_low, from_high, from_next = low[:, :1], high[:, :1], to_y_next(ratio)

    def own(k):
        return f32(pieces[k - EARLY - ALONE]) * ratio[None]

    def theirs(value, factor):
        return f32(value) * factor[None]

    e, f = to_z(e, 1), to_z(f, -1)
    g, h = to_z(left, 1), to_z(right, -1)
    from_next = after(from_next, g, h)
    c, d, e, f = after(c, g, h), after(d, g, h), after(e, g, h), after(f, g, h)
    third = (
        bf(own(8) + theirs(e, from_low)),
        bf(own(9) + theirs(c, from_next)),
        bf(own(10) + theirs(d, from_next)),
        bf(own(11) + theirs(f, from_high)),
        bf(own(12) + f32(g)),
        bf(own(13) + f32(h)),
    )
    others = (
        to_z(third[0], 1), to_z(third[1], 1),
        to_z(third[2], -1), to_z(third[3], -1),
        to_y_next(third[4]), to_y_next(third[5]),
    )
    total = ratio + from_next
    total = total + to_z(total, 2)
    total = total + to_z(total, 1)
    grad_gate, grad_up, grad_down = last_sum(pieces, others, ratio, total)

    part = [value[i : i + rows] for value in (near, far) for i in range(0, 4 * rows, rows)]
    far_0, far_1 = to_x(part[6], 1), to_x(part[7], -1)
    up_1, down_0 = to_x(part[5], 1), to_x(part[1], -1)
    up_0, down_1 = bf(f32(part[2]) + f32(far_0)), bf(f32(part[4]) + f32(far_1))
    up_0, down_1 = to_x(up_0, 1), to_x(down_1, -1)
    up_1, down_1 = after(up_1, *third), after(down_1, *third)
    other = bf(f32(part[3]) + f32(up_1) + f32(down_1))
    other = to_y_half(other)
    grad_tokens = bf(f32(part[0]) + f32(up_0) + f32(down_0) + f32(other))[None]
    return (grad_tokens, grad_gate, grad_up, grad_down)


def solution(mesh):
    return jax.shard_map(
        step,
        mesh=mesh,
        in_specs=(
            P("lang", "fsdp", None),
            P("lang", "fsdp", None),
            P("lang", None),
            P(None, "fsdp"),
            P(None, "fsdp"),
            P("fsdp", None),
        ),
        out_specs=(
            P("lang", "fsdp", None),
            P("lang", "fsdp"),
            P("lang", "fsdp"),
            P("fsdp", "lang"),
        ),
        check_vma=False,
    )
```

```python
import functools

import jax
import jax.numpy as jnp
from jax import lax
from jax.experimental import pallas as pl
from jax.experimental.pallas import tpu as pltpu
from jax.sharding import PartitionSpec as P


epsilon = 1e-06
INTERPRET = False
VMEM = (64 << 20) - 400000
VMEM_SMALL = 16 << 20

PLACES = ((0, 0), (-1, 0), (1, 0), (0, 1), (-1, 1), (1, 1), (2, 0), (2, 1))
BATCHES = ((0, 1, 2, 3), (4, 5, 6), (7,))
PIECES = (
    (2, 1, 0), (2, 1, 1), (1, 1, 1), (-1, 1, 0), (2, 0, 0), (2, 0, 1),
    (1, 1, 0), (-1, 1, 1), (1, 0, 0), (1, 0, 1), (-1, 0, 0), (-1, 0, 1),
    (0, 1, 0), (0, 1, 1), (0, 0, 0), (0, 0, 1),
)
EARLY = 4
ALONE = 4


def fsdp_pairs(dx, dy, dc):
    return [
        (y * 8 + x * 2 + c, (y ^ dy) * 8 + (x + dx) % 4 * 2 + (c ^ dc))
        for y in range(2)
        for x in range(4)
        for c in range(2)
    ]


def lang_pairs(dz, dy):
    return [(z * 2 + y, (z + dz) % 4 * 2 + (y ^ dy)) for z in range(4) for y in range(2)]


def to_x(value, step):
    return lax.ppermute(value, "fsdp", fsdp_pairs(step, 0, 0))


def to_y_half(value):
    return lax.ppermute(value, "fsdp", fsdp_pairs(0, 1, 0))


def to_core(value):
    return lax.ppermute(value, "fsdp", fsdp_pairs(0, 0, 1))


def to_z(value, step):
    return lax.ppermute(value, "lang", lang_pairs(step, 0))


def to_y_next(value):
    return lax.ppermute(value, "lang", lang_pairs(0, 1))


def after(value, *others):
    return lax.optimization_barrier((value, *others))[0]


def forward_kernel(n, *refs):
    toks, outs = refs[:n], refs[n : 2 * n]
    wg, wu, wd, inv, ggu_ref, hid_ref, tok_ref, out_ref, gate, up, back = refs[2 * n :]
    step = pl.program_id(0)
    features = jnp.concatenate([r[...] for r in toks], axis=0)
    upstream = jnp.concatenate([r[...] for r in outs], axis=0)
    tok_ref[...] = features
    out_ref[...] = upstream

    @pl.when(step == 0)
    def _():
        gate[...] = jnp.zeros_like(gate)
        up[...] = jnp.zeros_like(up)
        back[...] = jnp.zeros_like(back)

    gate[...] += jnp.dot(features, wg[...], preferred_element_type=jnp.float32)
    up[...] += jnp.dot(features, wu[...], preferred_element_type=jnp.float32)
    back[...] += contract_cols(upstream, wd[...])

    @pl.when(step == pl.num_programs(0) - 1)
    def _():
        width = gate.shape[1]
        inverse = inv[...]
        gate_pre = gate[...]
        up_pre = up[...]
        sig = 1.0 / (1.0 + jnp.exp(-gate_pre))
        act = gate_pre * sig
        hid_ref[...] = (act * up_pre * inverse).astype(hid_ref.dtype)
        hid_grad = back[...] * inverse
        gate_grad = hid_grad * up_pre * sig * (1.0 + gate_pre * (1.0 - sig))
        ggu_ref[:, :width] = gate_grad.astype(ggu_ref.dtype)
        ggu_ref[:, width:] = (hid_grad * act).astype(ggu_ref.dtype)


def forward(toks, outs, w_gate, w_up, w_down, inverse):
    n = len(toks)
    rows, depth = toks[0].shape
    hid = w_gate.shape[1]
    block = min(1024, depth)
    act = pl.BlockSpec((rows, block), lambda k: (0, k))
    wide = pl.BlockSpec((block, hid), lambda k: (k, 0))
    return pl.pallas_call(
        functools.partial(forward_kernel, n),
        name="forward",
        grid=(depth // block,),
        in_specs=[act] * (2 * n) + [wide, wide,
                  pl.BlockSpec((hid, block), lambda k: (0, k)),
                  pl.BlockSpec((n * rows, 1), lambda k: (0, 0))],
        out_specs=[pl.BlockSpec((n * rows, 2 * hid), lambda k: (0, 0)),
                   pl.BlockSpec((n * rows, hid), lambda k: (0, 0))]
        + [pl.BlockSpec((n * rows, block), lambda k: (0, k))] * 2,
        out_shape=[jax.ShapeDtypeStruct((n * rows, 2 * hid), jnp.bfloat16),
                   jax.ShapeDtypeStruct((n * rows, hid), jnp.bfloat16)]
        + [jax.ShapeDtypeStruct((n * rows, depth), jnp.bfloat16)] * 2,
        scratch_shapes=[pltpu.VMEM((n * rows, hid), jnp.float32)] * 3,
        compiler_params=pltpu.CompilerParams(
            dimension_semantics=("arbitrary",), vmem_limit_bytes=VMEM),
        interpret=INTERPRET,
    )(*toks, *outs, w_gate, w_up, w_down, inverse)


def input_kernel(n, *refs):
    ggus, (wg, wu, own, theirs) = refs[:n], refs[n:]
    hid = wg.shape[1]
    half = [r.shape[0] // 2 for r in ggus]
    ggu = jnp.concatenate(
        [r[:h] for r, h in zip(ggus, half)] + [r[h:] for r, h in zip(ggus, half)], axis=0
    )
    total = contract_cols(ggu[:, :hid], wg[...]) + contract_cols(ggu[:, hid:], wu[...])
    size = own.shape[0]
    own[...] = bf(total[:size])
    theirs[...] = bf(total[size:])


def input_gradient(ggus, w_gate, w_up):
    depth, hid = w_gate.shape
    block = min(1024, depth)
    size = sum(g.shape[0] for g in ggus) // 2
    wide = pl.BlockSpec((block, hid), lambda k: (k, 0))
    return pl.pallas_call(
        functools.partial(input_kernel, len(ggus)),
        name="input",
        grid=(depth // block,),
        in_specs=[pl.BlockSpec(g.shape, lambda k: (0, 0)) for g in ggus] + [wide, wide],
        out_specs=[pl.BlockSpec((size, block), lambda k: (0, k))] * 2,
        out_shape=[jax.ShapeDtypeStruct((size, depth), jnp.bfloat16)] * 2,
        compiler_params=pltpu.CompilerParams(
            dimension_semantics=("arbitrary",), vmem_limit_bytes=VMEM),
        interpret=INTERPRET,
    )(*ggus, w_gate, w_up)


def relay_kernel(own_a, own_b, a, b, ratio, low, high, left, right):
    factor = ratio[:, :1]
    for own, value, other, out in ((own_a, a, low, left), (own_b, b, high, right)):
        scale = other[:, :1]
        for m in range(3):
            out[m] = bf(f32(own[m]) * factor + f32(value[m]) * scale)


def relay(*arrays):
    whole = [pl.BlockSpec(v.shape, lambda k, n=v.ndim: (0,) * n) for v in arrays]
    return pl.pallas_call(
        relay_kernel,
        name="relay",
        grid=(1,),
        in_specs=whole,
        out_specs=whole[:2],
        out_shape=[jax.ShapeDtypeStruct(arrays[0].shape, jnp.bfloat16)] * 2,
        compiler_params=pltpu.CompilerParams(vmem_limit_bytes=VMEM_SMALL),
        interpret=INTERPRET,
    )(*arrays)


def join_kernel(pieces, a, b, ratio, left, right):
    factor = ratio[:, :1]
    for half, (value, out) in enumerate(((a, left), (b, right))):
        for m in range(3):
            out[m] = bf(f32(pieces[half, m]) * factor + f32(value[m]))


def join(pieces, first, a, b, ratio):
    _, _, hid, block = pieces.shape
    whole = [pl.BlockSpec(v.shape, lambda k, n=v.ndim: (0,) * n) for v in (a, b, ratio)]
    return pl.pallas_call(
        join_kernel,
        name="join",
        grid=(1,),
        in_specs=[pl.BlockSpec((2, 3, hid, block), lambda k: (first // 2, 0, 0, 0))] + whole,
        out_specs=whole[:2],
        out_shape=[jax.ShapeDtypeStruct(a.shape, jnp.bfloat16)] * 2,
        compiler_params=pltpu.CompilerParams(vmem_limit_bytes=VMEM),
        interpret=INTERPRET,
    )(pieces, a, b, ratio)


def last_kernel(pieces, l0, l1, r0, r1, n0, n1, ratio, total, gate, up, down):
    block = pieces.shape[3]
    factor, divisor = ratio[...], total[...]
    for half, group in enumerate(((l0, r0, n0), (l1, r1, n1))):
        at = half * block
        for m, ref in enumerate((gate, up, down)):
            value = f32(pieces[half, m]) * factor
            for other in group:
                value += f32(other[m])
            value = value / divisor
            if m == 2:
                ref[:, at : at + block] = bf(value)
            else:
                ref[at : at + block, :] = bf(value.T)


def last_sum(pieces, others, ratio, total):
    count, _, hid, block = pieces.shape
    whole = [pl.BlockSpec(a.shape, lambda k, n=a.ndim: (0,) * n) for a in (*others, ratio, total)]
    shapes = [(2 * block, hid), (2 * block, hid), (hid, 2 * block)]
    return pl.pallas_call(
        last_kernel,
        name="last",
        grid=(1,),
        in_specs=[pl.BlockSpec((2, 3, hid, block), lambda k: (count // 2 - 1, 0, 0, 0))] + whole,
        out_specs=[pl.BlockSpec(shape, lambda k: (0, 0)) for shape in shapes],
        out_shape=[jax.ShapeDtypeStruct(shape, jnp.bfloat16) for shape in shapes],
        compiler_params=pltpu.CompilerParams(vmem_limit_bytes=VMEM_SMALL),
        interpret=INTERPRET,
    )(pieces, *others, ratio, total)


def gradient_step(ggu_t, hid_t, toks, outs, write, moment):
    hid = hid_t.shape[0]
    features = jnp.concatenate([r[...] for r in toks], axis=0)
    upstream = jnp.concatenate([r[...] for r in outs], axis=0)
    first = jnp.dot(ggu_t[...], features, preferred_element_type=jnp.float32)
    second = jnp.dot(hid_t[...], upstream, preferred_element_type=jnp.float32)
    write(jnp.stack([bf(first[:hid]), bf(first[hid:]), bf(second)]))
    lanes = moment.shape[1]
    total = jnp.zeros(moment.shape, jnp.float32)
    for i in range(0, first.shape[1], lanes):
        a = first[:hid, i : i + lanes]
        b = first[hid:, i : i + lanes]
        c = second[:, i : i + lanes]
        total += a * a + b * b + c * c
    moment[...] += total


def to_one(step, alone, rest, value):
    for i, ref in enumerate(alone):
        @pl.when(step == i)
        def _():
            ref[...] = value

    if rest is not None:
        @pl.when(step >= len(alone))
        def _():
            rest[0] = value


def early_kernel(m, n, place, *refs):
    toks, outs = refs[:m], refs[m : 2 * m]
    ggus, hids = refs[2 * m : 2 * m + n], refs[2 * m + n : 2 * m + 2 * n]
    alone, (ggu_t, hid_t, moment) = refs[2 * m + 2 * n : -3], refs[-3:]
    step = pl.program_id(0)

    @pl.when(step == 0)
    def _():
        ggu = jnp.concatenate([r[...] for r in ggus], axis=0).astype(jnp.float32)
        ggu_t[...] = ggu.T.astype(ggu_t.dtype)
        hidden = jnp.concatenate([r[...] for r in hids], axis=0).astype(jnp.float32)
        hid_t[...] = hidden.T.astype(hid_t.dtype)
        moment[...] = jnp.zeros_like(moment)

    gradient_step(ggu_t, hid_t, toks, outs, functools.partial(to_one, step, alone, None), moment)


def late_kernel(m, depth, place, *refs):
    toks, outs = refs[:m], refs[m : 2 * m]
    ggu_t, hid_t, begun = refs[2 * m : 2 * m + 3]
    alone, (pieces, ratio, moment) = refs[2 * m + 3 : -3], refs[-3:]
    step = pl.program_id(0)

    @pl.when(step == 0)
    def _():
        moment[...] = begun[...]

    gradient_step(ggu_t, hid_t, toks, outs, functools.partial(to_one, step, alone, pieces), moment)

    @pl.when(step == pl.num_programs(0) - 1)
    def _():
        summed = jnp.sum(moment[...], axis=1, keepdims=True) / (3.0 * depth) + epsilon
        ratio[...] = jnp.broadcast_to(1.0 / summed, ratio.shape)


def same(array):
    zeros = (0,) * array.ndim
    return pl.BlockSpec(array.shape, lambda k, p: zeros)


def gradients_early(place, toks, outs, ggus, hids):
    n = len(ggus)
    depth, hid = toks[0].shape[1], hids[0].shape[1]
    rows = sum(t.shape[0] for t in toks)
    block = depth // len(PIECES)
    acts = [pl.BlockSpec((a.shape[0], block), lambda k, p: (0, p[k])) for a in (*toks, *outs)]
    out_shape = [
        *[jax.ShapeDtypeStruct((3, hid, block), jnp.bfloat16)] * EARLY,
        jax.ShapeDtypeStruct((2 * hid, rows), jnp.bfloat16),
        jax.ShapeDtypeStruct((hid, rows), jnp.bfloat16),
        jax.ShapeDtypeStruct((hid, min(128, block)), jnp.float32),
    ]
    return pl.pallas_call(
        functools.partial(early_kernel, len(toks), n),
        name="early",
        grid_spec=pltpu.PrefetchScalarGridSpec(
            num_scalar_prefetch=1,
            grid=(EARLY,),
            in_specs=acts + [same(a) for a in (*ggus, *hids)],
            out_specs=[same(a) for a in out_shape],
        ),
        out_shape=out_shape,
        compiler_params=pltpu.CompilerParams(
            dimension_semantics=("arbitrary",), vmem_limit_bytes=VMEM),
        interpret=INTERPRET,
    )(place, *toks, *outs, *ggus, *hids)


def gradients_late(place, toks, outs, ggu_t, hid_t, moment):
    depth, hid = toks[0].shape[1], hid_t.shape[0]
    block = depth // len(PIECES)
    late = len(PIECES) - EARLY
    alone = [jax.ShapeDtypeStruct((3, hid, block), jnp.bfloat16)] * ALONE
    acts = [pl.BlockSpec((a.shape[0], block), lambda k, p: (0, p[k])) for a in (*toks, *outs)]
    ratio = jax.ShapeDtypeStruct((hid, 128), jnp.float32)
    return pl.pallas_call(
        functools.partial(late_kernel, len(toks), depth),
        name="late",
        grid_spec=pltpu.PrefetchScalarGridSpec(
            num_scalar_prefetch=1,
            grid=(late,),
            in_specs=acts + [same(a) for a in (ggu_t, hid_t, moment)],
            out_specs=[same(a) for a in alone] + [
                pl.BlockSpec((1, 3, hid, block), lambda k, p: (jnp.maximum(k - ALONE, 0), 0, 0, 0)),
                same(ratio)],
            scratch_shapes=[pltpu.VMEM(moment.shape, jnp.float32)],
        ),
        out_shape=alone
        + [jax.ShapeDtypeStruct((late - ALONE, 3, hid, block), jnp.bfloat16), ratio],
        compiler_params=pltpu.CompilerParams(
            dimension_semantics=("arbitrary",), vmem_limit_bytes=VMEM),
        interpret=INTERPRET,
    )(place, *toks, *outs, ggu_t, hid_t, moment)


def contract_cols(left, right):
    return lax.dot_general(
        left, right, (((1,), (1,)), ((), ())), preferred_element_type=jnp.float32
    )


def bf(value):
    return value.astype(jnp.bfloat16)


def f32(value):
    return value.astype(jnp.float32)


def step(tokens, grad_out, doc_ids, w_gate, w_up, w_down):
    rows = tokens.shape[1]
    lang, fsdp = lax.axis_index("lang"), lax.axis_index("fsdp")
    z, y_lo = lang // 2, lang % 2
    y_hi, x, core = fsdp // 8, fsdp // 2 % 4, fsdp % 2

    t, o = {}, {}
    t[0], o[0] = tokens[0], grad_out[0]
    t[1], t[2], t[3] = to_x(t[0], 1), to_x(t[0], -1), to_y_half(t[0])
    o[1], o[2], o[3] = to_x(o[0], 1), to_x(o[0], -1), to_y_half(o[0])

    segment = doc_ids[0]
    same_document = (segment[:, None] == segment[None, :]).astype(jnp.float32)
    inverse = (1.0 / jnp.sum(same_document, axis=1)).reshape(16, rows)
    order = [(k, dc) for batch in BATCHES for dc in (0, 1) for k in batch]
    source = jnp.stack(
        [(y_hi ^ PLACES[k][1]) * 8 + (x + PLACES[k][0]) % 4 * 2 + (core ^ dc) for k, dc in order]
    )
    chosen = source[:, None] == jnp.arange(16)[None, :]
    inverse = jnp.sum(jnp.where(chosen[:, :, None], inverse[None], 0.0), axis=1)
    inverse = inverse.reshape(16 * rows, 1)
    target = jnp.stack([((z + dz) % 4 * 2 + (y_lo ^ dy)) * 2 + half for dz, dy, half in PIECES])
    target = target.astype(jnp.int32)

    t[4], t[5], t[6] = to_y_half(t[1]), to_x(t[3], -1), to_x(t[1], 1)
    o[5], o[4], o[6] = to_y_half(o[2]), to_x(o[3], 1), to_x(o[2], -1)

    t[7], o[7] = to_x(t[4], 1), to_x(o[5], -1)

    toks, outs, ggus, hids = [], [], [], []
    at = 0
    for batch in BATCHES:
        tok, out = [t[k] for k in batch], [o[k] for k in batch]
        tok += [to_core(v) for v in tok]
        out += [to_core(v) for v in out]
        size = rows * len(tok)
        ggu, hidden, tok, out = forward(
            tok, out, w_gate, w_up, w_down, inverse[at : at + size])
        at += size
        toks.append(tok)
        outs.append(out)
        ggus.append(ggu)
        hids.append(hidden)
    *first, ggu_t, hid_t, moment = gradients_early(target[:EARLY], toks, outs, ggus, hids)
    a, b = to_z(first[0], 1), to_z(first[1], -1)
    c, d = to_y_next(first[2]), to_y_next(first[3])
    far, far_p = input_gradient([after(ggus[1], moment), ggus[2]], w_gate, w_up)
    far_p, moment = lax.optimization_barrier((far_p, moment))
    far_p = to_core(far_p)
    far = bf(f32(far) + f32(far_p))
    e, f, own_g, own_h, pieces, ratio = gradients_late(target[EARLY:], toks, outs, ggu_t, hid_t, moment)
    low, high = to_z(ratio, 1), to_z(ratio, -1)
    left, right = relay(own_g, own_h, a, b, ratio, low, high)
    ratio_lanes, ratio = ratio, ratio[:, :1]
    from_low, from_high, from_next = low[:, :1], high[:, :1], to_y_next(ratio)

    def own(k):
        return f32(pieces[k - EARLY - ALONE]) * ratio[None]

    def theirs(value, factor):
        return f32(value) * factor[None]

    e, f = to_z(e, 1), to_z(f, -1)
    g, h = to_z(left, 1), to_z(right, -1)
    third_y = join(pieces, 12 - EARLY - ALONE, g, h, ratio_lanes)
    from_next = after(from_next, g, h)
    third = (
        bf(own(8) + theirs(e, from_low)),
        bf(own(9) + theirs(c, from_next)),
        bf(own(10) + theirs(d, from_next)),
        bf(own(11) + theirs(f, from_high)),
    )
    others = (
        to_z(third[0], 1), to_z(third[1], 1),
        to_z(third[2], -1), to_z(third[3], -1),
        to_y_next(third_y[0]), to_y_next(third_y[1]),
    )
    total = ratio + from_next
    total = total + to_z(total, 1) + to_z(total, -1) + to_z(total, 2)
    grad_gate, grad_up, grad_down = last_sum(pieces, others, ratio, total)

    near, near_p = input_gradient([after(ggus[0], left)], w_gate, w_up)
    near = bf(f32(near) + f32(to_core(near_p)))
    part = [value[i : i + rows] for value in (near, far) for i in range(0, 4 * rows, rows)]
    far_0, far_1 = to_x(part[6], 1), to_x(part[7], -1)
    up_1, down_0 = to_x(part[5], 1), to_x(part[1], -1)
    up_0, down_1 = bf(f32(part[2]) + f32(far_0)), bf(f32(part[4]) + f32(far_1))
    up_0, down_1 = to_x(up_0, 1), to_x(down_1, -1)
    up_1, down_1 = after(up_1, *third), after(down_1, *third)
    other = bf(f32(part[3]) + f32(up_1) + f32(down_1))
    other = to_y_half(other)
    grad_tokens = bf(f32(part[0]) + f32(up_0) + f32(down_0) + f32(other))[None]
    return (grad_tokens, grad_gate, grad_up, grad_down)


def solution(mesh):
    return jax.shard_map(
        step,
        mesh=mesh,
        in_specs=(
            P("lang", "fsdp", None),
            P("lang", "fsdp", None),
            P("lang", None),
            P(None, "fsdp"),
            P(None, "fsdp"),
            P("fsdp", None),
        ),
        out_specs=(
            P("lang", "fsdp", None),
            P("lang", "fsdp"),
            P("lang", "fsdp"),
            P("fsdp", "lang"),
        ),
        check_vma=False,
    )
```

```python
import functools

import jax
import jax.numpy as jnp
from jax import lax
from jax.experimental import pallas as pl
from jax.experimental.pallas import tpu as pltpu
from jax.sharding import PartitionSpec as P


epsilon = 1e-06
INTERPRET = False
VMEM = (64 << 20) - 400000
VMEM_SMALL = 16 << 20

PLACES = ((0, 0), (-1, 0), (1, 0), (0, 1), (-1, 1), (1, 1), (2, 0), (2, 1))
BATCHES = ((0, 1, 2, 3), (4, 5, 6), (7,))
PIECES = (
    (2, 1, 0), (2, 1, 1), (1, 1, 1), (-1, 1, 0), (2, 0, 0), (2, 0, 1),
    (1, 1, 0), (-1, 1, 1), (1, 0, 1), (-1, 0, 0), (1, 0, 0), (-1, 0, 1),
    (0, 1, 0), (0, 1, 1), (0, 0, 0), (0, 0, 1),
)
EARLY = 4
ALONE = 6


def fsdp_pairs(dx, dy, dc):
    return [
        (y * 8 + x * 2 + c, (y ^ dy) * 8 + (x + dx) % 4 * 2 + (c ^ dc))
        for y in range(2)
        for x in range(4)
        for c in range(2)
    ]


def lang_pairs(dz, dy):
    return [(z * 2 + y, (z + dz) % 4 * 2 + (y ^ dy)) for z in range(4) for y in range(2)]


def to_x(value, step):
    return lax.ppermute(value, "fsdp", fsdp_pairs(step, 0, 0))


def to_y_half(value):
    return lax.ppermute(value, "fsdp", fsdp_pairs(0, 1, 0))


def to_core(value):
    return lax.ppermute(value, "fsdp", fsdp_pairs(0, 0, 1))


def to_z(value, step):
    return lax.ppermute(value, "lang", lang_pairs(step, 0))


def to_y_next(value):
    return lax.ppermute(value, "lang", lang_pairs(0, 1))


def after(value, *others):
    return lax.optimization_barrier((value, *others))[0]


def forward_kernel(n, *refs):
    toks, outs = refs[:n], refs[n : 2 * n]
    wg, wu, wd, inv, ggu_ref, hid_ref, tok_ref, out_ref, gate, up, back = refs[2 * n :]
    step = pl.program_id(0)
    features = jnp.concatenate([r[...] for r in toks], axis=0)
    upstream = jnp.concatenate([r[...] for r in outs], axis=0)
    tok_ref[...] = features
    out_ref[...] = upstream

    @pl.when(step == 0)
    def _():
        gate[...] = jnp.zeros_like(gate)
        up[...] = jnp.zeros_like(up)
        back[...] = jnp.zeros_like(back)

    gate[...] += jnp.dot(features, wg[...], preferred_element_type=jnp.float32)
    up[...] += jnp.dot(features, wu[...], preferred_element_type=jnp.float32)
    back[...] += contract_cols(upstream, wd[...])

    @pl.when(step == pl.num_programs(0) - 1)
    def _():
        width = gate.shape[1]
        inverse = inv[...]
        gate_pre = gate[...]
        up_pre = up[...]
        sig = 1.0 / (1.0 + jnp.exp(-gate_pre))
        act = gate_pre * sig
        hid_ref[...] = (act * up_pre * inverse).astype(hid_ref.dtype)
        hid_grad = back[...] * inverse
        gate_grad = hid_grad * up_pre * sig * (1.0 + gate_pre * (1.0 - sig))
        ggu_ref[:, :width] = gate_grad.astype(ggu_ref.dtype)
        ggu_ref[:, width:] = (hid_grad * act).astype(ggu_ref.dtype)


def forward(toks, outs, w_gate, w_up, w_down, inverse):
    n = len(toks)
    rows, depth = toks[0].shape
    hid = w_gate.shape[1]
    block = min(1024, depth)
    act = pl.BlockSpec((rows, block), lambda k: (0, k))
    wide = pl.BlockSpec((block, hid), lambda k: (k, 0))
    return pl.pallas_call(
        functools.partial(forward_kernel, n),
        name="forward",
        grid=(depth // block,),
        in_specs=[act] * (2 * n) + [wide, wide,
                  pl.BlockSpec((hid, block), lambda k: (0, k)),
                  pl.BlockSpec((n * rows, 1), lambda k: (0, 0))],
        out_specs=[pl.BlockSpec((n * rows, 2 * hid), lambda k: (0, 0)),
                   pl.BlockSpec((n * rows, hid), lambda k: (0, 0))]
        + [pl.BlockSpec((n * rows, block), lambda k: (0, k))] * 2,
        out_shape=[jax.ShapeDtypeStruct((n * rows, 2 * hid), jnp.bfloat16),
                   jax.ShapeDtypeStruct((n * rows, hid), jnp.bfloat16)]
        + [jax.ShapeDtypeStruct((n * rows, depth), jnp.bfloat16)] * 2,
        scratch_shapes=[pltpu.VMEM((n * rows, hid), jnp.float32)] * 3,
        compiler_params=pltpu.CompilerParams(
            dimension_semantics=("arbitrary",), vmem_limit_bytes=VMEM),
        interpret=INTERPRET,
    )(*toks, *outs, w_gate, w_up, w_down, inverse)


def input_kernel(n, *refs):
    ggus, (wg, wu, own, theirs) = refs[:n], refs[n:]
    hid = wg.shape[1]
    half = [r.shape[0] // 2 for r in ggus]
    ggu = jnp.concatenate(
        [r[:h] for r, h in zip(ggus, half)] + [r[h:] for r, h in zip(ggus, half)], axis=0
    )
    total = contract_cols(ggu[:, :hid], wg[...]) + contract_cols(ggu[:, hid:], wu[...])
    size = own.shape[0]
    own[...] = bf(total[:size])
    theirs[...] = bf(total[size:])


def input_gradient(ggus, w_gate, w_up):
    depth, hid = w_gate.shape
    block = min(1024, depth)
    size = sum(g.shape[0] for g in ggus) // 2
    wide = pl.BlockSpec((block, hid), lambda k: (k, 0))
    return pl.pallas_call(
        functools.partial(input_kernel, len(ggus)),
        name="input",
        grid=(depth // block,),
        in_specs=[pl.BlockSpec(g.shape, lambda k: (0, 0)) for g in ggus] + [wide, wide],
        out_specs=[pl.BlockSpec((size, block), lambda k: (0, k))] * 2,
        out_shape=[jax.ShapeDtypeStruct((size, depth), jnp.bfloat16)] * 2,
        compiler_params=pltpu.CompilerParams(
            dimension_semantics=("arbitrary",), vmem_limit_bytes=VMEM),
        interpret=INTERPRET,
    )(*ggus, w_gate, w_up)


def relay_kernel(own_a, own_b, a, b, ratio, low, high, left, right):
    factor = ratio[:, :1]
    for own, value, other, out in ((own_a, a, low, left), (own_b, b, high, right)):
        scale = other[:, :1]
        for m in range(3):
            out[m] = bf(f32(own[m]) * factor + f32(value[m]) * scale)


def relay(*arrays):
    whole = [pl.BlockSpec(v.shape, lambda k, n=v.ndim: (0,) * n) for v in arrays]
    return pl.pallas_call(
        relay_kernel,
        name="relay",
        grid=(1,),
        in_specs=whole,
        out_specs=whole[:2],
        out_shape=[jax.ShapeDtypeStruct(arrays[0].shape, jnp.bfloat16)] * 2,
        compiler_params=pltpu.CompilerParams(vmem_limit_bytes=VMEM_SMALL),
        interpret=INTERPRET,
    )(*arrays)


def join_kernel(pieces, a, b, ratio, left, right):
    factor = ratio[:, :1]
    for half, (value, out) in enumerate(((a, left), (b, right))):
        for m in range(3):
            out[m] = bf(f32(pieces[half, m]) * factor + f32(value[m]))


def join(pieces, first, a, b, ratio):
    _, _, hid, block = pieces.shape
    whole = [pl.BlockSpec(v.shape, lambda k, n=v.ndim: (0,) * n) for v in (a, b, ratio)]
    return pl.pallas_call(
        join_kernel,
        name="join",
        grid=(1,),
        in_specs=[pl.BlockSpec((2, 3, hid, block), lambda k: (first // 2, 0, 0, 0))] + whole,
        out_specs=whole[:2],
        out_shape=[jax.ShapeDtypeStruct(a.shape, jnp.bfloat16)] * 2,
        compiler_params=pltpu.CompilerParams(vmem_limit_bytes=VMEM),
        interpret=INTERPRET,
    )(pieces, a, b, ratio)


def last_kernel(pieces, l0, l1, r0, r1, n0, n1, ratio, total, gate, up, down):
    block = pieces.shape[3]
    factor, divisor = ratio[...], total[...]
    for half, group in enumerate(((l0, r0, n0), (l1, r1, n1))):
        at = half * block
        for m, ref in enumerate((gate, up, down)):
            value = f32(pieces[half, m]) * factor
            for other in group:
                value += f32(other[m])
            value = value / divisor
            if m == 2:
                ref[:, at : at + block] = bf(value)
            else:
                ref[at : at + block, :] = bf(value.T)


def last_sum(pieces, others, ratio, total):
    count, _, hid, block = pieces.shape
    whole = [pl.BlockSpec(a.shape, lambda k, n=a.ndim: (0,) * n) for a in (*others, ratio, total)]
    shapes = [(2 * block, hid), (2 * block, hid), (hid, 2 * block)]
    return pl.pallas_call(
        last_kernel,
        name="last",
        grid=(1,),
        in_specs=[pl.BlockSpec((2, 3, hid, block), lambda k: (count // 2 - 1, 0, 0, 0))] + whole,
        out_specs=[pl.BlockSpec(shape, lambda k: (0, 0)) for shape in shapes],
        out_shape=[jax.ShapeDtypeStruct(shape, jnp.bfloat16) for shape in shapes],
        compiler_params=pltpu.CompilerParams(vmem_limit_bytes=VMEM_SMALL),
        interpret=INTERPRET,
    )(pieces, *others, ratio, total)


def gradient_step(ggu_t, hid_t, toks, outs, write, moment):
    hid = hid_t.shape[0]
    features = jnp.concatenate([r[...] for r in toks], axis=0)
    upstream = jnp.concatenate([r[...] for r in outs], axis=0)
    first = jnp.dot(ggu_t[...], features, preferred_element_type=jnp.float32)
    second = jnp.dot(hid_t[...], upstream, preferred_element_type=jnp.float32)
    write(jnp.stack([bf(first[:hid]), bf(first[hid:]), bf(second)]))
    lanes = moment.shape[1]
    total = jnp.zeros(moment.shape, jnp.float32)
    for i in range(0, first.shape[1], lanes):
        a = first[:hid, i : i + lanes]
        b = first[hid:, i : i + lanes]
        c = second[:, i : i + lanes]
        total += a * a + b * b + c * c
    moment[...] += total


def to_one(step, alone, rest, value):
    for i, ref in enumerate(alone):
        @pl.when(step == i)
        def _():
            ref[...] = value

    if rest is not None:
        @pl.when(step >= len(alone))
        def _():
            rest[0] = value


def early_kernel(m, n, place, *refs):
    toks, outs = refs[:m], refs[m : 2 * m]
    ggus, hids = refs[2 * m : 2 * m + n], refs[2 * m + n : 2 * m + 2 * n]
    alone, (ggu_t, hid_t, moment) = refs[2 * m + 2 * n : -3], refs[-3:]
    step = pl.program_id(0)

    @pl.when(step == 0)
    def _():
        ggu = jnp.concatenate([r[...] for r in ggus], axis=0).astype(jnp.float32)
        ggu_t[...] = ggu.T.astype(ggu_t.dtype)
        hidden = jnp.concatenate([r[...] for r in hids], axis=0).astype(jnp.float32)
        hid_t[...] = hidden.T.astype(hid_t.dtype)
        moment[...] = jnp.zeros_like(moment)

    gradient_step(ggu_t, hid_t, toks, outs, functools.partial(to_one, step, alone, None), moment)


def late_kernel(m, depth, place, *refs):
    toks, outs = refs[:m], refs[m : 2 * m]
    ggu_t, hid_t, begun = refs[2 * m : 2 * m + 3]
    alone, (pieces, ratio, moment) = refs[2 * m + 3 : -3], refs[-3:]
    step = pl.program_id(0)

    @pl.when(step == 0)
    def _():
        moment[...] = begun[...]

    gradient_step(ggu_t, hid_t, toks, outs, functools.partial(to_one, step, alone, pieces), moment)

    @pl.when(step == pl.num_programs(0) - 1)
    def _():
        summed = jnp.sum(moment[...], axis=1, keepdims=True) / (3.0 * depth) + epsilon
        ratio[...] = jnp.broadcast_to(1.0 / summed, ratio.shape)


def same(array):
    zeros = (0,) * array.ndim
    return pl.BlockSpec(array.shape, lambda k, p: zeros)


def gradients_early(place, toks, outs, ggus, hids):
    n = len(ggus)
    depth, hid = toks[0].shape[1], hids[0].shape[1]
    rows = sum(t.shape[0] for t in toks)
    block = depth // len(PIECES)
    acts = [pl.BlockSpec((a.shape[0], block), lambda k, p: (0, p[k])) for a in (*toks, *outs)]
    out_shape = [
        *[jax.ShapeDtypeStruct((3, hid, block), jnp.bfloat16)] * EARLY,
        jax.ShapeDtypeStruct((2 * hid, rows), jnp.bfloat16),
        jax.ShapeDtypeStruct((hid, rows), jnp.bfloat16),
        jax.ShapeDtypeStruct((hid, min(128, block)), jnp.float32),
    ]
    return pl.pallas_call(
        functools.partial(early_kernel, len(toks), n),
        name="early",
        grid_spec=pltpu.PrefetchScalarGridSpec(
            num_scalar_prefetch=1,
            grid=(EARLY,),
            in_specs=acts + [same(a) for a in (*ggus, *hids)],
            out_specs=[same(a) for a in out_shape],
        ),
        out_shape=out_shape,
        compiler_params=pltpu.CompilerParams(
            dimension_semantics=("arbitrary",), vmem_limit_bytes=VMEM),
        interpret=INTERPRET,
    )(place, *toks, *outs, *ggus, *hids)


def gradients_late(place, toks, outs, ggu_t, hid_t, moment):
    depth, hid = toks[0].shape[1], hid_t.shape[0]
    block = depth // len(PIECES)
    late = len(PIECES) - EARLY
    alone = [jax.ShapeDtypeStruct((3, hid, block), jnp.bfloat16)] * ALONE
    acts = [pl.BlockSpec((a.shape[0], block), lambda k, p: (0, p[k])) for a in (*toks, *outs)]
    ratio = jax.ShapeDtypeStruct((hid, 128), jnp.float32)
    return pl.pallas_call(
        functools.partial(late_kernel, len(toks), depth),
        name="late",
        grid_spec=pltpu.PrefetchScalarGridSpec(
            num_scalar_prefetch=1,
            grid=(late,),
            in_specs=acts + [same(a) for a in (ggu_t, hid_t, moment)],
            out_specs=[same(a) for a in alone] + [
                pl.BlockSpec((1, 3, hid, block), lambda k, p: (jnp.maximum(k - ALONE, 0), 0, 0, 0)),
                same(ratio)],
            scratch_shapes=[pltpu.VMEM(moment.shape, jnp.float32)],
        ),
        out_shape=alone
        + [jax.ShapeDtypeStruct((late - ALONE, 3, hid, block), jnp.bfloat16), ratio],
        compiler_params=pltpu.CompilerParams(
            dimension_semantics=("arbitrary",), vmem_limit_bytes=VMEM),
        interpret=INTERPRET,
    )(place, *toks, *outs, ggu_t, hid_t, moment)


def contract_cols(left, right):
    return lax.dot_general(
        left, right, (((1,), (1,)), ((), ())), preferred_element_type=jnp.float32
    )


def bf(value):
    return value.astype(jnp.bfloat16)


def f32(value):
    return value.astype(jnp.float32)


def step(tokens, grad_out, doc_ids, w_gate, w_up, w_down):
    rows = tokens.shape[1]
    lang, fsdp = lax.axis_index("lang"), lax.axis_index("fsdp")
    z, y_lo = lang // 2, lang % 2
    y_hi, x, core = fsdp // 8, fsdp // 2 % 4, fsdp % 2

    t, o = {}, {}
    t[0], o[0] = tokens[0], grad_out[0]
    t[1], t[2], t[3] = to_x(t[0], 1), to_x(t[0], -1), to_y_half(t[0])
    o[1], o[2], o[3] = to_x(o[0], 1), to_x(o[0], -1), to_y_half(o[0])

    segment = doc_ids[0]
    same_document = (segment[:, None] == segment[None, :]).astype(jnp.float32)
    inverse = (1.0 / jnp.sum(same_document, axis=1)).reshape(16, rows)
    order = [(k, dc) for batch in BATCHES for dc in (0, 1) for k in batch]
    source = jnp.stack(
        [(y_hi ^ PLACES[k][1]) * 8 + (x + PLACES[k][0]) % 4 * 2 + (core ^ dc) for k, dc in order]
    )
    chosen = source[:, None] == jnp.arange(16)[None, :]
    inverse = jnp.sum(jnp.where(chosen[:, :, None], inverse[None], 0.0), axis=1)
    inverse = inverse.reshape(16 * rows, 1)
    target = jnp.stack([((z + dz) % 4 * 2 + (y_lo ^ dy)) * 2 + half for dz, dy, half in PIECES])
    target = target.astype(jnp.int32)

    t[4], t[5], t[6] = to_y_half(t[1]), to_x(t[3], -1), to_x(t[1], 1)
    o[5], o[4], o[6] = to_y_half(o[2]), to_x(o[3], 1), to_x(o[2], -1)

    t[7], o[7] = to_x(t[4], 1), to_x(o[5], -1)

    toks, outs, ggus, hids = [], [], [], []
    at = 0
    for batch in BATCHES:
        tok, out = [t[k] for k in batch], [o[k] for k in batch]
        tok += [to_core(v) for v in tok]
        out += [to_core(v) for v in out]
        size = rows * len(tok)
        ggu, hidden, tok, out = forward(
            tok, out, w_gate, w_up, w_down, inverse[at : at + size])
        at += size
        toks.append(tok)
        outs.append(out)
        ggus.append(ggu)
        hids.append(hidden)
    *first, ggu_t, hid_t, moment = gradients_early(target[:EARLY], toks, outs, ggus, hids)
    a, b = to_z(first[0], 1), to_z(first[1], -1)
    c, d = to_y_next(first[2]), to_y_next(first[3])
    far, far_p = input_gradient([after(ggus[1], moment), ggus[2]], w_gate, w_up)
    far_p, moment = lax.optimization_barrier((far_p, moment))
    far_p = to_core(far_p)
    far = bf(f32(far) + f32(far_p))
    e, f, own_g, own_h, own_l, own_r, pieces, ratio = gradients_late(target[EARLY:], toks, outs, ggu_t, hid_t, moment)
    low, high = to_z(ratio, 1), to_z(ratio, -1)
    beside = to_y_next(ratio)
    left, right = relay(own_g, own_h, a, b, ratio, low, high)
    left_1, right_0 = relay(own_l, own_r, c, d, ratio, beside, beside)
    ratio_lanes, ratio = ratio, ratio[:, :1]
    from_low, from_high, from_next = low[:, :1], high[:, :1], beside[:, :1]

    def own(k):
        return f32(pieces[k - EARLY - ALONE]) * ratio[None]

    def theirs(value, factor):
        return f32(value) * factor[None]

    g, h = to_z(left, 1), to_z(right, -1)
    e, f = to_z(e, 1), to_z(f, -1)
    left_1, right_0 = to_z(left_1, 1), to_z(right_0, -1)
    third_y = join(pieces, 12 - EARLY - ALONE, g, h, ratio_lanes)
    from_next = after(from_next, left)
    third = bf(own(10) + theirs(e, from_low)), bf(own(11) + theirs(f, from_high))
    others = (
        to_z(third[0], 1), left_1, right_0, to_z(third[1], -1),
        to_y_next(third_y[0]), to_y_next(third_y[1]),
    )
    total = ratio + from_next
    total = total + to_z(total, 1) + to_z(total, -1) + to_z(total, 2)
    grad_gate, grad_up, grad_down = last_sum(pieces, others, ratio, total)

    near, near_p = input_gradient([after(ggus[0], left)], w_gate, w_up)
    near = bf(f32(near) + f32(to_core(near_p)))
    part = [value[i : i + rows] for value in (near, far) for i in range(0, 4 * rows, rows)]
    far_0, far_1 = to_x(part[6], 1), to_x(part[7], -1)
    up_1 = to_x(part[5], 1)
    down_1 = bf(f32(part[4]) + f32(far_1))
    down_1 = to_x(down_1, -1)
    up_0 = bf(f32(part[2]) + f32(far_0))
    up_0, down_0 = to_x(up_0, 1), to_x(part[1], -1)
    up_1, down_1 = after(up_1, *third_y), after(down_1, *third_y)
    other = bf(f32(part[3]) + f32(up_1) + f32(down_1))
    other = to_y_half(other)
    grad_tokens = bf(f32(part[0]) + f32(up_0) + f32(down_0) + f32(other))[None]
    return (grad_tokens, grad_gate, grad_up, grad_down)


def solution(mesh):
    return jax.shard_map(
        step,
        mesh=mesh,
        in_specs=(
            P("lang", "fsdp", None),
            P("lang", "fsdp", None),
            P("lang", None),
            P(None, "fsdp"),
            P(None, "fsdp"),
            P("fsdp", None),
        ),
        out_specs=(
            P("lang", "fsdp", None),
            P("lang", "fsdp"),
            P("lang", "fsdp"),
            P("fsdp", "lang"),
        ),
        check_vma=False,
    )
```

```python
import functools

import jax
import jax.numpy as jnp
from jax import lax
from jax.experimental import pallas as pl
from jax.experimental.pallas import tpu as pltpu
from jax.sharding import PartitionSpec as P


epsilon = 1e-06
INTERPRET = False
VMEM = (64 << 20) - 400000
VMEM_SMALL = 16 << 20

PLACES = ((0, 0), (-1, 0), (1, 0), (0, 1), (-1, 1), (1, 1), (2, 0), (2, 1))
BATCHES = ((0, 1, 2, 3), (4, 5, 6), (7,))
PIECES = (
    (2, 1, 0), (2, 1, 1), (1, 1, 1), (-1, 1, 0), (2, 0, 0), (2, 0, 1),
    (1, 1, 0), (-1, 1, 1), (1, 0, 1), (-1, 0, 0), (1, 0, 0), (-1, 0, 1),
    (0, 1, 0), (0, 1, 1), (0, 0, 0), (0, 0, 1),
)
EARLY = 4
ALONE = 6


def fsdp_pairs(dx, dy, dc):
    return [
        (y * 8 + x * 2 + c, (y ^ dy) * 8 + (x + dx) % 4 * 2 + (c ^ dc))
        for y in range(2)
        for x in range(4)
        for c in range(2)
    ]


def lang_pairs(dz, dy):
    return [(z * 2 + y, (z + dz) % 4 * 2 + (y ^ dy)) for z in range(4) for y in range(2)]


def to_x(value, step):
    return lax.ppermute(value, "fsdp", fsdp_pairs(step, 0, 0))


def to_y_half(value):
    return lax.ppermute(value, "fsdp", fsdp_pairs(0, 1, 0))


def to_core(value):
    return lax.ppermute(value, "fsdp", fsdp_pairs(0, 0, 1))


def to_z(value, step):
    return lax.ppermute(value, "lang", lang_pairs(step, 0))


def to_y_next(value):
    return lax.ppermute(value, "lang", lang_pairs(0, 1))


def after(value, *others):
    return lax.optimization_barrier((value, *others))[0]


def forward_kernel(n, *refs):
    toks, outs = refs[:n], refs[n : 2 * n]
    wg, wu, wd, inv, ggu_ref, hid_ref, tok_ref, out_ref, gate, up, back = refs[2 * n :]
    step = pl.program_id(0)
    features = jnp.concatenate([r[...] for r in toks], axis=0)
    upstream = jnp.concatenate([r[...] for r in outs], axis=0)
    tok_ref[...] = features
    out_ref[...] = upstream

    @pl.when(step == 0)
    def _():
        gate[...] = jnp.zeros_like(gate)
        up[...] = jnp.zeros_like(up)
        back[...] = jnp.zeros_like(back)

    gate[...] += jnp.dot(features, wg[...], preferred_element_type=jnp.float32)
    up[...] += jnp.dot(features, wu[...], preferred_element_type=jnp.float32)
    back[...] += contract_cols(upstream, wd[...])

    @pl.when(step == pl.num_programs(0) - 1)
    def _():
        width = gate.shape[1]
        inverse = inv[...]
        gate_pre = gate[...]
        up_pre = up[...]
        sig = 1.0 / (1.0 + jnp.exp(-gate_pre))
        act = gate_pre * sig
        hid_ref[...] = (act * up_pre * inverse).astype(hid_ref.dtype)
        hid_grad = back[...] * inverse
        gate_grad = hid_grad * up_pre * sig * (1.0 + gate_pre * (1.0 - sig))
        ggu_ref[:, :width] = gate_grad.astype(ggu_ref.dtype)
        ggu_ref[:, width:] = (hid_grad * act).astype(ggu_ref.dtype)


def forward(toks, outs, w_gate, w_up, w_down, inverse):
    n = len(toks)
    rows, depth = toks[0].shape
    hid = w_gate.shape[1]
    block = min(1024, depth)
    act = pl.BlockSpec((rows, block), lambda k: (0, k))
    wide = pl.BlockSpec((block, hid), lambda k: (k, 0))
    return pl.pallas_call(
        functools.partial(forward_kernel, n),
        name="forward",
        grid=(depth // block,),
        in_specs=[act] * (2 * n) + [wide, wide,
                  pl.BlockSpec((hid, block), lambda k: (0, k)),
                  pl.BlockSpec((n * rows, 1), lambda k: (0, 0))],
        out_specs=[pl.BlockSpec((n * rows, 2 * hid), lambda k: (0, 0)),
                   pl.BlockSpec((n * rows, hid), lambda k: (0, 0))]
        + [pl.BlockSpec((n * rows, block), lambda k: (0, k))] * 2,
        out_shape=[jax.ShapeDtypeStruct((n * rows, 2 * hid), jnp.bfloat16),
                   jax.ShapeDtypeStruct((n * rows, hid), jnp.bfloat16)]
        + [jax.ShapeDtypeStruct((n * rows, depth), jnp.bfloat16)] * 2,
        scratch_shapes=[pltpu.VMEM((n * rows, hid), jnp.float32)] * 3,
        compiler_params=pltpu.CompilerParams(
            dimension_semantics=("arbitrary",), vmem_limit_bytes=VMEM),
        interpret=INTERPRET,
    )(*toks, *outs, w_gate, w_up, w_down, inverse)


def input_kernel(n, *refs):
    ggus, (wg, wu, own, theirs) = refs[:n], refs[n:]
    hid = wg.shape[1]
    half = [r.shape[0] // 2 for r in ggus]
    ggu = jnp.concatenate(
        [r[:h] for r, h in zip(ggus, half)] + [r[h:] for r, h in zip(ggus, half)], axis=0
    )
    total = contract_cols(ggu[:, :hid], wg[...]) + contract_cols(ggu[:, hid:], wu[...])
    size = own.shape[0]
    own[...] = bf(total[:size])
    theirs[...] = bf(total[size:])


def input_gradient(ggus, w_gate, w_up):
    depth, hid = w_gate.shape
    block = min(1024, depth)
    size = sum(g.shape[0] for g in ggus) // 2
    wide = pl.BlockSpec((block, hid), lambda k: (k, 0))
    return pl.pallas_call(
        functools.partial(input_kernel, len(ggus)),
        name="input",
        grid=(depth // block,),
        in_specs=[pl.BlockSpec(g.shape, lambda k: (0, 0)) for g in ggus] + [wide, wide],
        out_specs=[pl.BlockSpec((size, block), lambda k: (0, k))] * 2,
        out_shape=[jax.ShapeDtypeStruct((size, depth), jnp.bfloat16)] * 2,
        compiler_params=pltpu.CompilerParams(
            dimension_semantics=("arbitrary",), vmem_limit_bytes=VMEM),
        interpret=INTERPRET,
    )(*ggus, w_gate, w_up)


def relay_kernel(own_a, own_b, a, b, ratio, low, high, left, right):
    factor = ratio[:, :1]
    for own, value, other, out in ((own_a, a, low, left), (own_b, b, high, right)):
        scale = other[:, :1]
        for m in range(3):
            out[m] = bf(f32(own[m]) * factor + f32(value[m]) * scale)


def relay(*arrays):
    whole = [pl.BlockSpec(v.shape, lambda k, n=v.ndim: (0,) * n) for v in arrays]
    return pl.pallas_call(
        relay_kernel,
        name="relay",
        grid=(1,),
        in_specs=whole,
        out_specs=whole[:2],
        out_shape=[jax.ShapeDtypeStruct(arrays[0].shape, jnp.bfloat16)] * 2,
        compiler_params=pltpu.CompilerParams(vmem_limit_bytes=VMEM),
        interpret=INTERPRET,
    )(*arrays)


def join_kernel(pieces, a, b, ratio, left, right):
    factor = ratio[:, :1]
    for half, (value, out) in enumerate(((a, left), (b, right))):
        for m in range(3):
            out[m] = bf(f32(pieces[half, m]) * factor + f32(value[m]))


def join(pieces, first, a, b, ratio):
    _, _, hid, block = pieces.shape
    whole = [pl.BlockSpec(v.shape, lambda k, n=v.ndim: (0,) * n) for v in (a, b, ratio)]
    return pl.pallas_call(
        join_kernel,
        name="join",
        grid=(1,),
        in_specs=[pl.BlockSpec((2, 3, hid, block), lambda k: (first // 2, 0, 0, 0))] + whole,
        out_specs=whole[:2],
        out_shape=[jax.ShapeDtypeStruct(a.shape, jnp.bfloat16)] * 2,
        compiler_params=pltpu.CompilerParams(vmem_limit_bytes=VMEM_SMALL),
        interpret=INTERPRET,
    )(pieces, a, b, ratio)


def last_kernel(pieces, l0, l1, r0, r1, n0, n1, ratio, total, gate, up, down):
    block = pieces.shape[3]
    factor, divisor = ratio[...], total[...]
    for half, group in enumerate(((l0, r0, n0), (l1, r1, n1))):
        at = half * block
        for m, ref in enumerate((gate, up, down)):
            value = f32(pieces[half, m]) * factor
            for other in group:
                value += f32(other[m])
            value = value / divisor
            if m == 2:
                ref[:, at : at + block] = bf(value)
            else:
                ref[at : at + block, :] = bf(value.T)


def last_sum(pieces, others, ratio, total):
    count, _, hid, block = pieces.shape
    whole = [pl.BlockSpec(a.shape, lambda k, n=a.ndim: (0,) * n) for a in (*others, ratio, total)]
    shapes = [(2 * block, hid), (2 * block, hid), (hid, 2 * block)]
    return pl.pallas_call(
        last_kernel,
        name="last",
        grid=(1,),
        in_specs=[pl.BlockSpec((2, 3, hid, block), lambda k: (count // 2 - 1, 0, 0, 0))] + whole,
        out_specs=[pl.BlockSpec(shape, lambda k: (0, 0)) for shape in shapes],
        out_shape=[jax.ShapeDtypeStruct(shape, jnp.bfloat16) for shape in shapes],
        compiler_params=pltpu.CompilerParams(vmem_limit_bytes=VMEM_SMALL),
        interpret=INTERPRET,
    )(pieces, *others, ratio, total)


def gradient_step(ggu_t, hid_t, toks, outs, write, moment):
    hid = hid_t.shape[0]
    features = jnp.concatenate([r[...] for r in toks], axis=0)
    upstream = jnp.concatenate([r[...] for r in outs], axis=0)
    first = jnp.dot(ggu_t[...], features, preferred_element_type=jnp.float32)
    second = jnp.dot(hid_t[...], upstream, preferred_element_type=jnp.float32)
    write(jnp.stack([bf(first[:hid]), bf(first[hid:]), bf(second)]))
    lanes = moment.shape[1]
    total = jnp.zeros(moment.shape, jnp.float32)
    for i in range(0, first.shape[1], lanes):
        a = first[:hid, i : i + lanes]
        b = first[hid:, i : i + lanes]
        c = second[:, i : i + lanes]
        total += a * a + b * b + c * c
    moment[...] += total


def to_one(step, alone, rest, value):
    for i, ref in enumerate(alone):
        @pl.when(step == i)
        def _():
            ref[...] = value

    if rest is not None:
        @pl.when(step >= len(alone))
        def _():
            rest[0] = value


def early_kernel(m, n, place, *refs):
    toks, outs = refs[:m], refs[m : 2 * m]
    ggus, hids = refs[2 * m : 2 * m + n], refs[2 * m + n : 2 * m + 2 * n]
    alone, (ggu_t, hid_t, moment) = refs[2 * m + 2 * n : -3], refs[-3:]
    step = pl.program_id(0)

    @pl.when(step == 0)
    def _():
        ggu = jnp.concatenate([r[...] for r in ggus], axis=0).astype(jnp.float32)
        ggu_t[...] = ggu.T.astype(ggu_t.dtype)
        hidden = jnp.concatenate([r[...] for r in hids], axis=0).astype(jnp.float32)
        hid_t[...] = hidden.T.astype(hid_t.dtype)
        moment[...] = jnp.zeros_like(moment)

    gradient_step(ggu_t, hid_t, toks, outs, functools.partial(to_one, step, alone, None), moment)


def late_kernel(m, depth, place, *refs):
    toks, outs = refs[:m], refs[m : 2 * m]
    ggu_t, hid_t, begun = refs[2 * m : 2 * m + 3]
    alone, (pieces, ratio, moment) = refs[2 * m + 3 : -3], refs[-3:]
    step = pl.program_id(0)

    @pl.when(step == 0)
    def _():
        moment[...] = begun[...]

    gradient_step(ggu_t, hid_t, toks, outs, functools.partial(to_one, step, alone, pieces), moment)

    @pl.when(step == pl.num_programs(0) - 1)
    def _():
        summed = jnp.sum(moment[...], axis=1, keepdims=True) / (3.0 * depth) + epsilon
        ratio[...] = jnp.broadcast_to(1.0 / summed, ratio.shape)


def same(array):
    zeros = (0,) * array.ndim
    return pl.BlockSpec(array.shape, lambda k, p: zeros)


def gradients_early(place, toks, outs, ggus, hids):
    n = len(ggus)
    depth, hid = toks[0].shape[1], hids[0].shape[1]
    rows = sum(t.shape[0] for t in toks)
    block = depth // len(PIECES)
    acts = [pl.BlockSpec((a.shape[0], block), lambda k, p: (0, p[k])) for a in (*toks, *outs)]
    out_shape = [
        *[jax.ShapeDtypeStruct((3, hid, block), jnp.bfloat16)] * EARLY,
        jax.ShapeDtypeStruct((2 * hid, rows), jnp.bfloat16),
        jax.ShapeDtypeStruct((hid, rows), jnp.bfloat16),
        jax.ShapeDtypeStruct((hid, min(128, block)), jnp.float32),
    ]
    return pl.pallas_call(
        functools.partial(early_kernel, len(toks), n),
        name="early",
        grid_spec=pltpu.PrefetchScalarGridSpec(
            num_scalar_prefetch=1,
            grid=(EARLY,),
            in_specs=acts + [same(a) for a in (*ggus, *hids)],
            out_specs=[same(a) for a in out_shape],
        ),
        out_shape=out_shape,
        compiler_params=pltpu.CompilerParams(
            dimension_semantics=("arbitrary",), vmem_limit_bytes=VMEM),
        interpret=INTERPRET,
    )(place, *toks, *outs, *ggus, *hids)


def gradients_late(place, toks, outs, ggu_t, hid_t, moment):
    depth, hid = toks[0].shape[1], hid_t.shape[0]
    block = depth // len(PIECES)
    late = len(PIECES) - EARLY
    alone = [jax.ShapeDtypeStruct((3, hid, block), jnp.bfloat16)] * ALONE
    acts = [pl.BlockSpec((a.shape[0], block), lambda k, p: (0, p[k])) for a in (*toks, *outs)]
    ratio = jax.ShapeDtypeStruct((hid, 128), jnp.float32)
    return pl.pallas_call(
        functools.partial(late_kernel, len(toks), depth),
        name="late",
        grid_spec=pltpu.PrefetchScalarGridSpec(
            num_scalar_prefetch=1,
            grid=(late,),
            in_specs=acts + [same(a) for a in (ggu_t, hid_t, moment)],
            out_specs=[same(a) for a in alone] + [
                pl.BlockSpec((1, 3, hid, block), lambda k, p: (jnp.maximum(k - ALONE, 0), 0, 0, 0)),
                same(ratio)],
            scratch_shapes=[pltpu.VMEM(moment.shape, jnp.float32)],
        ),
        out_shape=alone
        + [jax.ShapeDtypeStruct((late - ALONE, 3, hid, block), jnp.bfloat16), ratio],
        compiler_params=pltpu.CompilerParams(
            dimension_semantics=("arbitrary",), vmem_limit_bytes=VMEM),
        interpret=INTERPRET,
    )(place, *toks, *outs, ggu_t, hid_t, moment)


def contract_cols(left, right):
    return lax.dot_general(
        left, right, (((1,), (1,)), ((), ())), preferred_element_type=jnp.float32
    )


def bf(value):
    return value.astype(jnp.bfloat16)


def f32(value):
    return value.astype(jnp.float32)


def step(tokens, grad_out, doc_ids, w_gate, w_up, w_down):
    rows = tokens.shape[1]
    lang, fsdp = lax.axis_index("lang"), lax.axis_index("fsdp")
    z, y_lo = lang // 2, lang % 2
    y_hi, x, core = fsdp // 8, fsdp // 2 % 4, fsdp % 2

    t, o = {}, {}
    t[0], o[0] = tokens[0], grad_out[0]
    t[1], t[2], t[3] = to_x(t[0], 1), to_x(t[0], -1), to_y_half(t[0])
    o[1], o[2], o[3] = to_x(o[0], 1), to_x(o[0], -1), to_y_half(o[0])

    segment = doc_ids[0]
    same_document = (segment[:, None] == segment[None, :]).astype(jnp.float32)
    inverse = (1.0 / jnp.sum(same_document, axis=1)).reshape(16, rows)
    order = [(k, dc) for batch in BATCHES for dc in (0, 1) for k in batch]
    source = jnp.stack(
        [(y_hi ^ PLACES[k][1]) * 8 + (x + PLACES[k][0]) % 4 * 2 + (core ^ dc) for k, dc in order]
    )
    chosen = source[:, None] == jnp.arange(16)[None, :]
    inverse = jnp.sum(jnp.where(chosen[:, :, None], inverse[None], 0.0), axis=1)
    inverse = inverse.reshape(16 * rows, 1)
    target = jnp.stack([((z + dz) % 4 * 2 + (y_lo ^ dy)) * 2 + half for dz, dy, half in PIECES])
    target = target.astype(jnp.int32)

    t[4], t[5], t[6] = to_y_half(t[1]), to_x(t[3], -1), to_x(t[1], 1)
    o[5], o[4], o[6] = to_y_half(o[2]), to_x(o[3], 1), to_x(o[2], -1)

    t[7], o[7] = to_x(t[4], 1), to_x(o[5], -1)

    toks, outs, ggus, hids = [], [], [], []
    at = 0
    for batch in BATCHES:
        tok, out = [t[k] for k in batch], [o[k] for k in batch]
        tok += [to_core(v) for v in tok]
        out += [to_core(v) for v in out]
        size = rows * len(tok)
        ggu, hidden, tok, out = forward(
            tok, out, w_gate, w_up, w_down, inverse[at : at + size])
        at += size
        toks.append(tok)
        outs.append(out)
        ggus.append(ggu)
        hids.append(hidden)
    near, near_p = input_gradient(ggus[:1], w_gate, w_up)
    near_p = to_core(near_p)

    *first, ggu_t, hid_t, moment = gradients_early(target[:EARLY], toks, outs, ggus, hids)
    a, b = to_z(first[0], 1), to_z(first[1], -1)
    c, d = to_y_next(first[2]), to_y_next(first[3])
    far, far_p = input_gradient([after(ggus[1], moment), ggus[2]], w_gate, w_up)
    far_p, moment = lax.optimization_barrier((far_p, moment))
    far_p = to_core(far_p)
    far = bf(f32(far) + f32(far_p))
    e, f, own_g, own_h, own_l, own_r, pieces, ratio = gradients_late(target[EARLY:], toks, outs, ggu_t, hid_t, moment)
    low, high = to_z(ratio, 1), to_z(ratio, -1)
    beside = to_y_next(ratio)
    left, right = relay(own_g, own_h, a, b, ratio, low, high)
    left_1, right_0 = relay(own_l, own_r, c, d, ratio, beside, beside)
    ratio_lanes, ratio = ratio, ratio[:, :1]
    from_low, from_high, from_next = low[:, :1], high[:, :1], beside[:, :1]

    def own(k):
        return f32(pieces[k - EARLY - ALONE]) * ratio[None]

    def theirs(value, factor):
        return f32(value) * factor[None]

    g, h = to_z(left, 1), to_z(right, -1)
    e, f = to_z(e, 1), to_z(f, -1)
    left_1, right_0 = to_z(left_1, 1), to_z(right_0, -1)
    third_y = join(pieces, 12 - EARLY - ALONE, g, h, ratio_lanes)
    from_next = after(from_next, left)
    third = bf(own(10) + theirs(e, from_low)), bf(own(11) + theirs(f, from_high))
    others = (
        to_z(third[0], 1), left_1, right_0, to_z(third[1], -1),
        to_y_next(third_y[0]), to_y_next(third_y[1]),
    )
    total = ratio + from_next
    total = total + to_z(total, 1) + to_z(total, -1) + to_z(total, 2)
    grad_gate, grad_up, grad_down = last_sum(pieces, others, ratio, total)

    near, near_p = after(near, *third_y), after(near_p, *third_y)
    near = bf(f32(near) + f32(near_p))
    part = [value[i : i + rows] for value in (near, far) for i in range(0, 4 * rows, rows)]
    far_0, far_1 = to_x(part[6], 1), to_x(part[7], -1)
    up_1 = to_x(part[5], 1)
    down_1 = bf(f32(part[4]) + f32(far_1))
    down_1 = to_x(down_1, -1)
    up_0 = bf(f32(part[2]) + f32(far_0))
    up_0, down_0 = to_x(up_0, 1), to_x(part[1], -1)
    up_1, down_1 = after(up_1, *third_y), after(down_1, *third_y)
    other = bf(f32(part[3]) + f32(up_1) + f32(down_1))
    other = to_y_half(other)
    grad_tokens = bf(f32(part[0]) + f32(up_0) + f32(down_0) + f32(other))[None]
    return (grad_tokens, grad_gate, grad_up, grad_down)


def solution(mesh):
    return jax.shard_map(
        step,
        mesh=mesh,
        in_specs=(
            P("lang", "fsdp", None),
            P("lang", "fsdp", None),
            P("lang", None),
            P(None, "fsdp"),
            P(None, "fsdp"),
            P("fsdp", None),
        ),
        out_specs=(
            P("lang", "fsdp", None),
            P("lang", "fsdp"),
            P("lang", "fsdp"),
            P("fsdp", "lang"),
        ),
        check_vma=False,
    )
```

```python
import functools

import jax
import jax.numpy as jnp
from jax import lax
from jax.experimental import pallas as pl
from jax.experimental.pallas import tpu as pltpu
from jax.sharding import PartitionSpec as P


epsilon = 1e-06
INTERPRET = False
VMEM = (64 << 20) - 400000
VMEM_SMALL = 16 << 20

PLACES = ((0, 0), (-1, 0), (1, 0), (0, 1), (-1, 1), (1, 1), (2, 0), (2, 1))
BATCHES = ((0, 1, 2, 3), (4, 5, 6), (7,))
PIECES = (
    (2, 1, 0), (2, 1, 1), (1, 1, 1), (-1, 1, 0), (2, 0, 0), (2, 0, 1),
    (1, 1, 0), (-1, 1, 1), (1, 0, 1), (-1, 0, 0), (1, 0, 0), (-1, 0, 1),
    (0, 1, 0), (0, 1, 1), (0, 0, 0), (0, 0, 1),
)
EARLY = 4
ALONE = 6


def fsdp_pairs(dx, dy, dc):
    return [
        (y * 8 + x * 2 + c, (y ^ dy) * 8 + (x + dx) % 4 * 2 + (c ^ dc))
        for y in range(2)
        for x in range(4)
        for c in range(2)
    ]


def lang_pairs(dz, dy):
    return [(z * 2 + y, (z + dz) % 4 * 2 + (y ^ dy)) for z in range(4) for y in range(2)]


def to_x(value, step):
    return lax.ppermute(value, "fsdp", fsdp_pairs(step, 0, 0))


def to_y_half(value):
    return lax.ppermute(value, "fsdp", fsdp_pairs(0, 1, 0))


def to_core(value):
    return lax.ppermute(value, "fsdp", fsdp_pairs(0, 0, 1))


def to_z(value, step):
    return lax.ppermute(value, "lang", lang_pairs(step, 0))


def to_y_next(value):
    return lax.ppermute(value, "lang", lang_pairs(0, 1))


def after(value, *others):
    return lax.optimization_barrier((value, *others))[0]


def forward_kernel(n, *refs):
    toks, outs = refs[:n], refs[n : 2 * n]
    wg, wu, wd, inv, ggu_ref, hid_ref, tok_ref, out_ref, gate, up, back = refs[2 * n :]
    step = pl.program_id(0)
    features = jnp.concatenate([r[...] for r in toks], axis=0)
    upstream = jnp.concatenate([r[...] for r in outs], axis=0)
    tok_ref[...] = features
    out_ref[...] = upstream

    @pl.when(step == 0)
    def _():
        gate[...] = jnp.zeros_like(gate)
        up[...] = jnp.zeros_like(up)
        back[...] = jnp.zeros_like(back)

    gate[...] += jnp.dot(features, wg[...], preferred_element_type=jnp.float32)
    up[...] += jnp.dot(features, wu[...], preferred_element_type=jnp.float32)
    back[...] += contract_cols(upstream, wd[...])

    @pl.when(step == pl.num_programs(0) - 1)
    def _():
        width = gate.shape[1]
        inverse = inv[...]
        gate_pre = gate[...]
        up_pre = up[...]
        sig = 1.0 / (1.0 + jnp.exp(-gate_pre))
        act = gate_pre * sig
        hid_ref[...] = (act * up_pre * inverse).astype(hid_ref.dtype)
        hid_grad = back[...] * inverse
        gate_grad = hid_grad * up_pre * sig * (1.0 + gate_pre * (1.0 - sig))
        ggu_ref[:, :width] = gate_grad.astype(ggu_ref.dtype)
        ggu_ref[:, width:] = (hid_grad * act).astype(ggu_ref.dtype)


def forward(toks, outs, w_gate, w_up, w_down, inverse):
    n = len(toks)
    rows, depth = toks[0].shape
    hid = w_gate.shape[1]
    block = min(1024, depth)
    act = pl.BlockSpec((rows, block), lambda k: (0, k))
    wide = pl.BlockSpec((block, hid), lambda k: (k, 0))
    return pl.pallas_call(
        functools.partial(forward_kernel, n),
        name="forward",
        grid=(depth // block,),
        in_specs=[act] * (2 * n) + [wide, wide,
                  pl.BlockSpec((hid, block), lambda k: (0, k)),
                  pl.BlockSpec((n * rows, 1), lambda k: (0, 0))],
        out_specs=[pl.BlockSpec((n * rows, 2 * hid), lambda k: (0, 0)),
                   pl.BlockSpec((n * rows, hid), lambda k: (0, 0))]
        + [pl.BlockSpec((n * rows, block), lambda k: (0, k))] * 2,
        out_shape=[jax.ShapeDtypeStruct((n * rows, 2 * hid), jnp.bfloat16),
                   jax.ShapeDtypeStruct((n * rows, hid), jnp.bfloat16)]
        + [jax.ShapeDtypeStruct((n * rows, depth), jnp.bfloat16)] * 2,
        scratch_shapes=[pltpu.VMEM((n * rows, hid), jnp.float32)] * 3,
        compiler_params=pltpu.CompilerParams(
            dimension_semantics=("arbitrary",), vmem_limit_bytes=VMEM),
        interpret=INTERPRET,
    )(*toks, *outs, w_gate, w_up, w_down, inverse)


def input_kernel(n, *refs):
    ggus, (wg, wu, own, theirs) = refs[:n], refs[n:]
    hid = wg.shape[1]
    half = [r.shape[0] // 2 for r in ggus]
    ggu = jnp.concatenate(
        [r[:h] for r, h in zip(ggus, half)] + [r[h:] for r, h in zip(ggus, half)], axis=0
    )
    total = contract_cols(ggu[:, :hid], wg[...]) + contract_cols(ggu[:, hid:], wu[...])
    size = own.shape[0]
    own[...] = bf(total[:size])
    theirs[...] = bf(total[size:])


def input_gradient(ggus, w_gate, w_up):
    depth, hid = w_gate.shape
    block = min(1024, depth)
    size = sum(g.shape[0] for g in ggus) // 2
    wide = pl.BlockSpec((block, hid), lambda k: (k, 0))
    return pl.pallas_call(
        functools.partial(input_kernel, len(ggus)),
        name="input",
        grid=(depth // block,),
        in_specs=[pl.BlockSpec(g.shape, lambda k: (0, 0)) for g in ggus] + [wide, wide],
        out_specs=[pl.BlockSpec((size, block), lambda k: (0, k))] * 2,
        out_shape=[jax.ShapeDtypeStruct((size, depth), jnp.bfloat16)] * 2,
        compiler_params=pltpu.CompilerParams(
            dimension_semantics=("arbitrary",), vmem_limit_bytes=VMEM),
        interpret=INTERPRET,
    )(*ggus, w_gate, w_up)


def relay_kernel(own_a, own_b, a, b, ratio, low, high, left, right):
    factor = ratio[:, :1]
    for own, value, other, out in ((own_a, a, low, left), (own_b, b, high, right)):
        scale = other[:, :1]
        for m in range(3):
            out[m] = bf(f32(own[m]) * factor + f32(value[m]) * scale)


def relay(*arrays):
    whole = [pl.BlockSpec(v.shape, lambda k, n=v.ndim: (0,) * n) for v in arrays]
    return pl.pallas_call(
        relay_kernel,
        name="relay",
        grid=(1,),
        in_specs=whole,
        out_specs=whole[:2],
        out_shape=[jax.ShapeDtypeStruct(arrays[0].shape, jnp.bfloat16)] * 2,
        compiler_params=pltpu.CompilerParams(vmem_limit_bytes=VMEM),
        interpret=INTERPRET,
    )(*arrays)


def join_kernel(pieces, a, b, ratio, left, right):
    factor = ratio[:, :1]
    for half, (value, out) in enumerate(((a, left), (b, right))):
        for m in range(3):
            out[m] = bf(f32(pieces[half, m]) * factor + f32(value[m]))


def join(pieces, first, a, b, ratio):
    _, _, hid, block = pieces.shape
    whole = [pl.BlockSpec(v.shape, lambda k, n=v.ndim: (0,) * n) for v in (a, b, ratio)]
    return pl.pallas_call(
        join_kernel,
        name="join",
        grid=(1,),
        in_specs=[pl.BlockSpec((2, 3, hid, block), lambda k: (first // 2, 0, 0, 0))] + whole,
        out_specs=whole[:2],
        out_shape=[jax.ShapeDtypeStruct(a.shape, jnp.bfloat16)] * 2,
        compiler_params=pltpu.CompilerParams(vmem_limit_bytes=VMEM_SMALL),
        interpret=INTERPRET,
    )(pieces, a, b, ratio)


def last_kernel(pieces, l0, l1, r0, r1, n0, n1, ratio, total, gate, up, down):
    block = pieces.shape[3]
    factor, divisor = ratio[...], total[...]
    for half, group in enumerate(((l0, r0, n0), (l1, r1, n1))):
        at = half * block
        for m, ref in enumerate((gate, up, down)):
            value = f32(pieces[half, m]) * factor
            for other in group:
                value += f32(other[m])
            value = value / divisor
            if m == 2:
                ref[:, at : at + block] = bf(value)
            else:
                ref[at : at + block, :] = bf(value.T)


def last_sum(pieces, others, ratio, total):
    count, _, hid, block = pieces.shape
    whole = [pl.BlockSpec(a.shape, lambda k, n=a.ndim: (0,) * n) for a in (*others, ratio, total)]
    shapes = [(2 * block, hid), (2 * block, hid), (hid, 2 * block)]
    return pl.pallas_call(
        last_kernel,
        name="last",
        grid=(1,),
        in_specs=[pl.BlockSpec((2, 3, hid, block), lambda k: (count // 2 - 1, 0, 0, 0))] + whole,
        out_specs=[pl.BlockSpec(shape, lambda k: (0, 0)) for shape in shapes],
        out_shape=[jax.ShapeDtypeStruct(shape, jnp.bfloat16) for shape in shapes],
        compiler_params=pltpu.CompilerParams(vmem_limit_bytes=VMEM_SMALL),
        interpret=INTERPRET,
    )(pieces, *others, ratio, total)


def gradient_step(ggu_t, hid_t, toks, outs, write, moment):
    hid = hid_t.shape[0]
    features = jnp.concatenate([r[...] for r in toks], axis=0)
    upstream = jnp.concatenate([r[...] for r in outs], axis=0)
    first = jnp.dot(ggu_t[...], features, preferred_element_type=jnp.float32)
    second = jnp.dot(hid_t[...], upstream, preferred_element_type=jnp.float32)
    write(jnp.stack([bf(first[:hid]), bf(first[hid:]), bf(second)]))
    lanes = moment.shape[1]
    total = jnp.zeros(moment.shape, jnp.float32)
    for i in range(0, first.shape[1], lanes):
        a = first[:hid, i : i + lanes]
        b = first[hid:, i : i + lanes]
        c = second[:, i : i + lanes]
        total += a * a + b * b + c * c
    moment[...] += total


def to_one(step, alone, rest, value):
    for i, ref in enumerate(alone):
        @pl.when(step == i)
        def _():
            ref[...] = value

    if rest is not None:
        @pl.when(step >= len(alone))
        def _():
            rest[0] = value


def early_kernel(m, n, place, *refs):
    toks, outs = refs[:m], refs[m : 2 * m]
    ggus, hids = refs[2 * m : 2 * m + n], refs[2 * m + n : 2 * m + 2 * n]
    alone, (ggu_t, hid_t, moment) = refs[2 * m + 2 * n : -3], refs[-3:]
    step = pl.program_id(0)

    @pl.when(step == 0)
    def _():
        ggu_t[...] = jnp.concatenate([r[...] for r in ggus], axis=0).T
        hid_t[...] = jnp.concatenate([r[...] for r in hids], axis=0).T
        moment[...] = jnp.zeros_like(moment)

    gradient_step(ggu_t, hid_t, toks, outs, functools.partial(to_one, step, alone, None), moment)


def late_kernel(m, depth, place, *refs):
    toks, outs = refs[:m], refs[m : 2 * m]
    ggu_t, hid_t, begun = refs[2 * m : 2 * m + 3]
    alone, (pieces, ratio, moment) = refs[2 * m + 3 : -3], refs[-3:]
    step = pl.program_id(0)

    @pl.when(step == 0)
    def _():
        moment[...] = begun[...]

    gradient_step(ggu_t, hid_t, toks, outs, functools.partial(to_one, step, alone, pieces), moment)

    @pl.when(step == pl.num_programs(0) - 1)
    def _():
        summed = jnp.sum(moment[...], axis=1, keepdims=True) / (3.0 * depth) + epsilon
        ratio[...] = jnp.broadcast_to(1.0 / summed, ratio.shape)


def same(array):
    zeros = (0,) * array.ndim
    return pl.BlockSpec(array.shape, lambda k, p: zeros)


def gradients_early(place, toks, outs, ggus, hids):
    n = len(ggus)
    depth, hid = toks[0].shape[1], hids[0].shape[1]
    rows = sum(t.shape[0] for t in toks)
    block = depth // len(PIECES)
    acts = [pl.BlockSpec((a.shape[0], block), lambda k, p: (0, p[k])) for a in (*toks, *outs)]
    out_shape = [
        *[jax.ShapeDtypeStruct((3, hid, block), jnp.bfloat16)] * EARLY,
        jax.ShapeDtypeStruct((2 * hid, rows), jnp.bfloat16),
        jax.ShapeDtypeStruct((hid, rows), jnp.bfloat16),
        jax.ShapeDtypeStruct((hid, min(128, block)), jnp.float32),
    ]
    return pl.pallas_call(
        functools.partial(early_kernel, len(toks), n),
        name="early",
        grid_spec=pltpu.PrefetchScalarGridSpec(
            num_scalar_prefetch=1,
            grid=(EARLY,),
            in_specs=acts + [same(a) for a in (*ggus, *hids)],
            out_specs=[same(a) for a in out_shape],
        ),
        out_shape=out_shape,
        compiler_params=pltpu.CompilerParams(
            dimension_semantics=("arbitrary",), vmem_limit_bytes=VMEM),
        interpret=INTERPRET,
    )(place, *toks, *outs, *ggus, *hids)


def gradients_late(place, toks, outs, ggu_t, hid_t, moment):
    depth, hid = toks[0].shape[1], hid_t.shape[0]
    block = depth // len(PIECES)
    late = len(PIECES) - EARLY
    alone = [jax.ShapeDtypeStruct((3, hid, block), jnp.bfloat16)] * ALONE
    acts = [pl.BlockSpec((a.shape[0], block), lambda k, p: (0, p[k])) for a in (*toks, *outs)]
    ratio = jax.ShapeDtypeStruct((hid, 128), jnp.float32)
    return pl.pallas_call(
        functools.partial(late_kernel, len(toks), depth),
        name="late",
        grid_spec=pltpu.PrefetchScalarGridSpec(
            num_scalar_prefetch=1,
            grid=(late,),
            in_specs=acts + [same(a) for a in (ggu_t, hid_t, moment)],
            out_specs=[same(a) for a in alone] + [
                pl.BlockSpec((1, 3, hid, block), lambda k, p: (jnp.maximum(k - ALONE, 0), 0, 0, 0)),
                same(ratio)],
            scratch_shapes=[pltpu.VMEM(moment.shape, jnp.float32)],
        ),
        out_shape=alone
        + [jax.ShapeDtypeStruct((late - ALONE, 3, hid, block), jnp.bfloat16), ratio],
        compiler_params=pltpu.CompilerParams(
            dimension_semantics=("arbitrary",), vmem_limit_bytes=VMEM),
        interpret=INTERPRET,
    )(place, *toks, *outs, ggu_t, hid_t, moment)


def contract_cols(left, right):
    return lax.dot_general(
        left, right, (((1,), (1,)), ((), ())), preferred_element_type=jnp.float32
    )


def bf(value):
    return value.astype(jnp.bfloat16)


def f32(value):
    return value.astype(jnp.float32)


def step(tokens, grad_out, doc_ids, w_gate, w_up, w_down):
    rows = tokens.shape[1]
    lang, fsdp = lax.axis_index("lang"), lax.axis_index("fsdp")
    z, y_lo = lang // 2, lang % 2
    y_hi, x, core = fsdp // 8, fsdp // 2 % 4, fsdp % 2

    t, o = {}, {}
    t[0], o[0] = tokens[0], grad_out[0]
    t[1], t[2], t[3] = to_x(t[0], 1), to_x(t[0], -1), to_y_half(t[0])
    o[1], o[2], o[3] = to_x(o[0], 1), to_x(o[0], -1), to_y_half(o[0])

    segment = doc_ids[0]
    same_document = (segment[:, None] == segment[None, :]).astype(jnp.float32)
    inverse = (1.0 / jnp.sum(same_document, axis=1)).reshape(16, rows)
    order = [(k, dc) for batch in BATCHES for dc in (0, 1) for k in batch]
    source = jnp.stack(
        [(y_hi ^ PLACES[k][1]) * 8 + (x + PLACES[k][0]) % 4 * 2 + (core ^ dc) for k, dc in order]
    )
    chosen = source[:, None] == jnp.arange(16)[None, :]
    inverse = jnp.sum(jnp.where(chosen[:, :, None], inverse[None], 0.0), axis=1)
    inverse = inverse.reshape(16 * rows, 1)
    target = jnp.stack([((z + dz) % 4 * 2 + (y_lo ^ dy)) * 2 + half for dz, dy, half in PIECES])
    target = target.astype(jnp.int32)

    t[4], t[5], t[6] = to_y_half(t[1]), to_x(t[3], -1), to_x(t[1], 1)
    o[5], o[4], o[6] = to_y_half(o[2]), to_x(o[3], 1), to_x(o[2], -1)

    t[7], o[7] = to_x(t[4], 1), to_x(o[5], -1)

    toks, outs, ggus, hids = [], [], [], []
    at = 0
    for batch in BATCHES:
        tok, out = [t[k] for k in batch], [o[k] for k in batch]
        tok += [to_core(v) for v in tok]
        out += [to_core(v) for v in out]
        size = rows * len(tok)
        ggu, hidden, tok, out = forward(
            tok, out, w_gate, w_up, w_down, inverse[at : at + size])
        at += size
        toks.append(tok)
        outs.append(out)
        ggus.append(ggu)
        hids.append(hidden)
    near, near_p = input_gradient(ggus[:1], w_gate, w_up)
    near_p = to_core(near_p)

    *first, ggu_t, hid_t, moment = gradients_early(target[:EARLY], toks, outs, ggus, hids)
    a, b = to_z(first[0], 1), to_z(first[1], -1)
    c, d = to_y_next(first[2]), to_y_next(first[3])
    far, far_p = input_gradient([after(ggus[1], moment), ggus[2]], w_gate, w_up)
    far_p = to_core(far_p)
    far = bf(f32(far) + f32(far_p))
    e, f, own_g, own_h, own_l, own_r, pieces, ratio = gradients_late(target[EARLY:], toks, outs, ggu_t, hid_t, moment)
    low, high = to_z(ratio, 1), to_z(ratio, -1)
    beside = to_y_next(ratio)
    left, right = relay(own_g, own_h, a, b, ratio, low, high)
    left_1, right_0 = relay(own_l, own_r, c, d, ratio, beside, beside)
    ratio_lanes, ratio = ratio, ratio[:, :1]
    from_low, from_high, from_next = low[:, :1], high[:, :1], beside[:, :1]

    def own(k):
        return f32(pieces[k - EARLY - ALONE]) * ratio[None]

    def theirs(value, factor):
        return f32(value) * factor[None]

    g, h = to_z(left, 1), to_z(right, -1)
    e, f = to_z(e, 1), to_z(f, -1)
    left_1, right_0 = to_z(left_1, 1), to_z(right_0, -1)
    third_y = join(pieces, 12 - EARLY - ALONE, g, h, ratio_lanes)
    from_next = after(from_next, left)
    third = bf(own(10) + theirs(e, from_low)), bf(own(11) + theirs(f, from_high))
    others = (
        to_z(third[0], 1), left_1, right_0, to_z(third[1], -1),
        to_y_next(third_y[0]), to_y_next(third_y[1]),
    )
    total = ratio + from_next
    total = total + to_z(total, 1) + to_z(total, -1) + to_z(total, 2)
    grad_gate, grad_up, grad_down = last_sum(pieces, others, ratio, total)

    near, near_p = after(near, *third_y), after(near_p, *third_y)
    near = bf(f32(near) + f32(near_p))
    part = [value[i : i + rows] for value in (near, far) for i in range(0, 4 * rows, rows)]
    far_0, far_1 = to_x(part[6], 1), to_x(part[7], -1)
    up_1 = to_x(part[5], 1)
    down_1 = bf(f32(part[4]) + f32(far_1))
    down_1 = to_x(down_1, -1)
    up_0 = bf(f32(part[2]) + f32(far_0))
    up_0, down_0 = to_x(up_0, 1), to_x(part[1], -1)
    up_1, down_1 = after(up_1, *third_y), after(down_1, *third_y)
    other = bf(f32(part[3]) + f32(up_1) + f32(down_1))
    other = to_y_half(other)
    grad_tokens = bf(f32(part[0]) + f32(up_0) + f32(down_0) + f32(other))[None]
    return (grad_tokens, grad_gate, grad_up, grad_down)


def solution(mesh):
    return jax.shard_map(
        step,
        mesh=mesh,
        in_specs=(
            P("lang", "fsdp", None),
            P("lang", "fsdp", None),
            P("lang", None),
            P(None, "fsdp"),
            P(None, "fsdp"),
            P("fsdp", None),
        ),
        out_specs=(
            P("lang", "fsdp", None),
            P("lang", "fsdp"),
            P("lang", "fsdp"),
            P("fsdp", "lang"),
        ),
        check_vma=False,
    )
```
